128 devices in a mesh: orient: 32 (over x, z, y_lo), slab: 4 (over y_hi, core).
Axes of the slice: x: 4, y: 4 (y_hi: 2, y_lo: 2; y = y_hi * 2 + y_lo), z: 4, core: 2. Of those that a mesh axis runs over, the one named last changes fastest.
Arguments:
- volume: bfloat16 [32, 512, 8192], P('orient', 'slab'), may hold values from 0 to 2
- rays: bfloat16 [8192, 8, 128], replicated, may hold values from -0.0234375 to 0.0234375
- band_start: int32 [8, 32], P(None, 'orient'), may hold values from 0 to 63
- band_len: int32 [8, 32], P(None, 'orient'), may hold values from 32 to 64
- slot_image: int32 [32], replicated, may hold values from 0 to 31, each once
- measured: float32 [32, 512, 128], P('orient', 'slab'), may hold values from -6 to 6
- relax: float32 [32], P('orient'), may hold values from 0.25 to 1
Outputs:
- updated: bfloat16 [32, 512, 8192], P('orient', 'slab')
- residual: float32 [32, 512, 128], P('orient', 'slab')
The draws below stay inside these ranges and needn't reach their ends.
Inputs may be any that keep to these rules, and one draw needn't show every extreme that they name: `slot_image`: every image number appears in exactly one slot. band_start + band_len stays below 128.
All inputs are finite; a program needn't handle non-finite values.
Results may differ from the reference program's by a relative error of at most 0.0055.
Values may be sent and summed in bfloat16 or wider, within the bound.
No kernel may reach another device: no remote copies, remote signals or barrier semaphores. Data moves between devices by JAX's collectives and lax.ppermute only.
A program may use at most 128 MiB of HBM per device.

```python
import math
import jax
import jax.numpy as jnp
from jax import lax

DW = 128
REFL = 8
FRAMES = 4
SWEEPS = 2
CELLS = 8192
ROWS = 512
ORIENTS = 32
IMAGES = 32


def place_ends(result, own_key, low, largest):
    place = [jax.random.randint(jax.random.fold_in(own_key, axis), (), 0, length) for axis, length in enumerate(result.shape)]
    longest = result.shape.index(max(result.shape))
    neighbour = place[:longest] + [(place[longest] + 1) % result.shape[longest]] + place[longest + 1:]
    return result.at[tuple(place)].set(low).at[tuple(neighbour)].set(largest)


def block_levels(stream_key, dims, pieces, least, largest):
    level, own = 1.0, jax.random.fold_in(stream_key, 6)
    for axis_at, shards_of in pieces:
        draws = jnp.exp(jax.random.uniform(jax.random.fold_in(own, axis_at), (shards_of,), jnp.float32, least / len(pieces), largest / len(pieces)))
        level = level * jnp.repeat(draws, dims[axis_at] // shards_of).reshape([-1 if axis == axis_at else 1 for axis in range(len(dims))])
    return level


def gaussian(stream_key, extent, spread, most, split=(), kind=jnp.bfloat16):
    entries = spread * jax.random.normal(stream_key, extent, jnp.float32)
    if split:
        entries = entries * block_levels(stream_key, extent, split, -0.22, 0.18)
    return jnp.clip(entries, -most, most).astype(kind)


def setup_inputs(seed: int = 0) -> dict:
    streams_of = jax.random.split(jax.random.key(seed), 8)
    volume = jnp.clip(2.0 * jax.random.uniform(streams_of[0], (ORIENTS, ROWS, CELLS), jnp.float32) ** block_levels(streams_of[0], (ORIENTS, ROWS, CELLS), ((0, 32), (1, 4)), -0.2, 0.2), 0.0, 2.0).astype(jnp.bfloat16)
    rays = gaussian(streams_of[1], (CELLS, REFL, DW), (CELLS * ORIENTS // FRAMES) ** -0.5, 0.0234375)
    band_start = place_ends(jax.random.randint(streams_of[2], (REFL, ORIENTS), 0, DW // 2), jax.random.fold_in(streams_of[2], 1), 0, (DW // 2) - 1).astype(jnp.int32)
    band_len = place_ends(jax.random.randint(streams_of[3], (REFL, ORIENTS), DW // 4, DW // 2 + 1), jax.random.fold_in(streams_of[3], 1), DW // 4, (DW // 2 + 1) - 1).astype(jnp.int32)
    slot_image = jax.random.permutation(streams_of[4], IMAGES).astype(jnp.int32)
    measured = gaussian(streams_of[5], (IMAGES, ROWS, DW), 1.0, 6.0, ((0, 32), (1, 4)), jnp.float32)
    relax = jnp.clip(jnp.exp(math.log(1.0) - 1.3862944 * jax.random.uniform(streams_of[6], (ORIENTS,), jnp.float32) ** block_levels(streams_of[6], (ORIENTS,), ((0, 32),), -0.2, 0.2)), 0.25, 1.0)
    return dict(volume=volume, rays=rays, band_start=band_start, band_len=band_len, slot_image=slot_image, measured=measured, relax=relax)


huber_delta = 0.5
sweep_rate = 0.2

def smooth_pass(extended, first_row, total_rows):
    middle = extended[:, 1:-1]
    row_count = middle.shape[1]
    global_rows = first_row + 1 + jnp.arange(row_count, dtype=jnp.int32)
    has_above = (global_rows > 0)[None, :, None]
    has_below = (global_rows < total_rows - 1)[None, :, None]
    from_above = jnp.clip(middle - extended[:, :-2], -huber_delta, huber_delta)
    from_below = jnp.clip(middle - extended[:, 2:], -huber_delta, huber_delta)
    row_flux = jnp.where(has_above, from_above, 0.0) + jnp.where(has_below, from_below, 0.0)
    return middle - sweep_rate * row_flux

def band_masks(band_start, band_len, detector):
    columns = jnp.arange(detector, dtype=jnp.int32)
    inside = (columns >= band_start[:, :, None]) & (columns < (band_start + band_len)[:, :, None])
    return inside.astype(jnp.float32)

def reference(volume, rays, band_start, band_len, slot_image, measured, relax):
    flat_rays = rays.reshape(CELLS, REFL * DW)
    band_mask = band_masks(band_start, band_len, DW)
    orient_ids = jnp.arange(ORIENTS, dtype=jnp.int32)
    reflections = jnp.arange(REFL, dtype=jnp.int32)
    frame_of = (orient_ids[:, None] + reflections[None, :]) % FRAMES
    frame_pick = (frame_of[:, :, None] == jnp.arange(FRAMES, dtype=jnp.int32)).astype(jnp.float32)

    def forward(total, orient_id):
        projected = jnp.dot(volume[orient_id], flat_rays, preferred_element_type=jnp.float32)
        projected = projected.reshape(ROWS, REFL, DW)
        term = jnp.einsum('kf,kd,rkd->kfrd', frame_pick[orient_id], band_mask[:, orient_id], projected)
        return (total + term, None)
    evolved = lax.scan(forward, jnp.zeros((REFL, FRAMES, ROWS, DW), jnp.float32), orient_ids)[0]
    evolved = evolved.reshape(IMAGES, ROWS, DW)
    residual = measured - evolved[slot_image]
    residual_sent = residual.astype(jnp.bfloat16)
    inverse = jnp.zeros((IMAGES,), jnp.int32).at[slot_image].set(jnp.arange(IMAGES, dtype=jnp.int32))
    by_image = residual_sent[inverse].reshape(REFL, FRAMES, ROWS, DW)
    step_gain = math.sqrt(CELLS * ORIENTS / (FRAMES * REFL * DW))
    rays_wide = rays.astype(jnp.float32)

    def backward(orient_id):
        picked = by_image[reflections, frame_of[orient_id]]
        masked = picked * band_mask[:, orient_id][:, None, :].astype(jnp.bfloat16)
        gradient = jnp.einsum('krd,ckd->rc', masked.astype(jnp.float32), rays_wide)
        density = volume[orient_id].astype(jnp.float32) + relax[orient_id] * step_gain * gradient
        for repeat in range(SWEEPS):
            extended = jnp.pad(density[None], ((0, 0), (1, 1), (0, 0)))
            density = smooth_pass(extended, -1, ROWS)[0]
        return density.astype(jnp.bfloat16)
    updated = lax.map(backward, orient_ids)
    return (updated, residual)
```

```python
import math

import jax
import jax.numpy as jnp
from jax import lax
from jax.experimental import pallas as pl
from jax.experimental.pallas import tpu as pltpu
from jax.sharding import PartitionSpec as P

FRAMES = 4
SWEEPS = 2
HALO = 16

huber_delta = 0.5
sweep_rate = 0.2

bf16 = jnp.bfloat16
f32 = jnp.float32


def project_kernel(vol_hbm, halo_ref, rays_hbm, mask_ref, proj_ref, flat_ref, vol_ref, buf, acc, vsem, rsem):
    chunk = buf.shape[0] // rsem.shape[0]
    chunks = rsem.shape[0]
    rows = vol_hbm.shape[0]
    refl, det = rays_hbm.shape[1:]

    def rays_copy(i):
        at = pl.ds(pl.multiple_of(i * chunk, chunk), chunk)
        return pltpu.make_async_copy(rays_hbm.at[at], buf.at[at], rsem.at[i])

    def vol_copy(i):
        at = pl.ds(pl.multiple_of(i * chunk, chunk), chunk)
        return pltpu.make_async_copy(vol_hbm.at[:, at], vol_ref.at[0:rows, at], vsem.at[i])

    for i in range(chunks):
        vol_copy(i).start()
        rays_copy(i).start()
    vol_ref[rows:, :] = halo_ref[...]
    acc[...] = jnp.zeros_like(acc)

    def step(i, carry):
        at = pl.ds(pl.multiple_of(i * chunk, chunk), chunk)
        vol_copy(i).wait()
        rays_copy(i).wait()
        flat = buf[at].reshape(chunk, refl * det)
        flat_ref[at, :] = flat
        acc[...] += jnp.dot(vol_ref[:, at], flat, preferred_element_type=f32)
        return carry

    lax.fori_loop(0, chunks, step, 0)
    for k in range(refl):
        proj_ref[k] = acc[:, k * det : (k + 1) * det] * mask_ref[k : k + 1, :]


def project(vol, halo, rays, mask, chunk=1024):
    rows, cells = vol.shape
    refl, det = rays.shape[1:]
    ext = rows + HALO
    vmem = pl.BlockSpec(memory_space=pltpu.VMEM)
    hbm = pl.BlockSpec(memory_space=pltpu.HBM)
    return pl.pallas_call(
        project_kernel,
        in_specs=[hbm, vmem, hbm, vmem],
        out_specs=(vmem, vmem, vmem),
        out_shape=(
            jax.ShapeDtypeStruct((refl, ext, det), f32),
            pltpu.VMEM((cells, refl * det), bf16),
            pltpu.VMEM((ext, cells), bf16),
        ),
        scratch_shapes=[
            pltpu.VMEM(rays.shape, bf16),
            pltpu.VMEM((ext, refl * det), f32),
            pltpu.SemaphoreType.DMA((cells // chunk,)),
            pltpu.SemaphoreType.DMA((cells // chunk,)),
        ],
        compiler_params=pltpu.CompilerParams(vmem_limit_bytes=24 << 20),
        name="project",
    )(vol, halo, rays, mask)


def update_kernel(img_ref, mask_ref, flat_ref, vol_ref, bound_ref, scale_ref, out_hbm, obuf, osem):
    refl = img_ref.shape[0]
    ext, cells = vol_ref.shape
    rows, chunk = obuf.shape[1:]
    img = jnp.concatenate([img_ref[k] * mask_ref[k : k + 1, :] for k in range(refl)], axis=1)
    bound = bound_ref[:, :1]
    scale = scale_ref[0]

    def out_copy(i, slot):
        at = pl.ds(pl.multiple_of(i * chunk, chunk), chunk)
        return pltpu.make_async_copy(obuf.at[slot], out_hbm.at[:, at], osem.at[slot])

    def step(i, carry):
        at = pl.ds(pl.multiple_of(i * chunk, chunk), chunk)
        slot = lax.rem(i, 2)
        gradient = lax.dot_general(
            img, flat_ref[at, :], (((1,), (1,)), ((), ())), preferred_element_type=f32
        )
        density = vol_ref[:, at].astype(f32) + scale * gradient
        for _ in range(SWEEPS):
            flux = pltpu.roll(density, ext - 1, 0) - density
            flux = jnp.minimum(jnp.maximum(flux, -bound), bound)
            density = density + sweep_rate * (flux - pltpu.roll(flux, 1, 0))

        @pl.when(i >= 2)
        def _():
            out_copy(i - 2, slot).wait()

        obuf[slot] = density[:rows].astype(bf16)
        out_copy(i, slot).start()
        return carry

    steps = cells // chunk
    lax.fori_loop(0, steps, step, 0)
    for i in range(steps - 2, steps):
        out_copy(i, i % 2).wait()


def update(img, mask, flat, vol_ext, bound, scale, chunk=1024):
    ext, cells = vol_ext.shape
    rows = ext - HALO
    vmem = pl.BlockSpec(memory_space=pltpu.VMEM)
    return pl.pallas_call(
        update_kernel,
        in_specs=[vmem] * 5 + [pl.BlockSpec(memory_space=pltpu.SMEM)],
        out_specs=pl.BlockSpec(memory_space=pltpu.HBM),
        out_shape=jax.ShapeDtypeStruct((rows, cells), bf16),
        scratch_shapes=[pltpu.VMEM((2, rows, chunk), bf16), pltpu.SemaphoreType.DMA((2,))],
        compiler_params=pltpu.CompilerParams(vmem_limit_bytes=24 << 20),
        name="update",
    )(img, mask, flat, vol_ext, bound, scale)


def local(volume, rays, band_start, band_len, slot_image, measured, relax):
    cells, refl, det = rays.shape
    rows = volume.shape[1]
    slabs = lax.axis_size("slab")
    orients = lax.axis_size("orient")
    orient = lax.axis_index("orient")
    slab = lax.axis_index("slab")
    members = orients // FRAMES
    classes = [[g * FRAMES + q for g in range(members)] for q in range(FRAMES)]
    vol = volume[0]
    meas = measured[0].astype(bf16)

    edge = jnp.concatenate([vol, meas], axis=1)
    above = lax.ppermute(edge[rows - 2 :], "slab", [(i, i + 1) for i in range(slabs - 1)])
    below = lax.ppermute(edge[:2], "slab", [(i + 1, i) for i in range(slabs - 1)])
    halo = jnp.concatenate([below, jnp.zeros((HALO - 4, cells + det), bf16), above], axis=0)
    meas_ext = jnp.concatenate([meas, halo[:, cells:]], axis=0)

    gathered = [meas_ext] + [
        lax.ppermute(meas_ext, "orient", [(o, o ^ s) for o in range(orients)]) for s in range(1, FRAMES)
    ]

    columns = jnp.arange(det, dtype=jnp.int32)
    inside = (columns >= band_start) & (columns < band_start + band_len)
    mask = inside.astype(f32)
    proj, flat, vol_ext = project(vol, halo[:, :cells], rays, mask)

    reflections = jnp.arange(refl, dtype=jnp.int32)
    wanted = reflections * FRAMES + (orient + reflections) % FRAMES
    part = proj
    for s in range(FRAMES):
        held = (wanted == slot_image[orient ^ s]).astype(f32)
        part = part - held[:, None, None] * gathered[s].astype(f32)[None]
    pieces = lax.all_to_all(
        part.astype(bf16), "orient", 0, 0, axis_index_groups=classes, tiled=True
    )
    own = (-jnp.sum(pieces.astype(f32), axis=0)).astype(bf16)
    images = lax.all_to_all(
        jnp.broadcast_to(own[None], (members, rows + HALO, det)),
        "orient", 0, 0, axis_index_groups=classes, tiled=True,
    )

    mine = slot_image[orient]
    source = ((mine % FRAMES - mine // FRAMES) ^ orient) % FRAMES
    residual = images[mine // FRAMES, :rows]
    for s in range(1, FRAMES):
        sent = images[slot_image[orient ^ s] // FRAMES, :rows]
        got = lax.ppermute(sent, "orient", [(o, o ^ s) for o in range(orients)])
        residual = jnp.where(source == s, got, residual)

    step_gain = math.sqrt(cells * orients / (FRAMES * refl * det))
    place = jnp.arange(rows + HALO, dtype=jnp.int32)[:, None]
    last = (place == rows - 1) & (slab == slabs - 1)
    first = (place == rows + HALO - 1) & (slab == 0)
    bound = jnp.broadcast_to(jnp.where(last | first, 0.0, huber_delta), (rows + HALO, det))
    updated = update(images, mask.astype(bf16), flat, vol_ext, bound, relax * step_gain)
    return (updated[None], residual.astype(f32)[None])


def solution(mesh):
    placed = (
        P("orient", "slab", None),
        P(),
        P(None, "orient"),
        P(None, "orient"),
        P(),
        P("orient", "slab", None),
        P("orient"),
    )
    return jax.shard_map(
        local,
        mesh=mesh,
        in_specs=placed,
        out_specs=(P("orient", "slab", None), P("orient", "slab", None)),
        check_vma=False,
    )
```

```python
import math

import jax
import jax.numpy as jnp
from jax import lax
from jax.experimental import pallas as pl
from jax.experimental.pallas import tpu as pltpu
from jax.sharding import PartitionSpec as P

FRAMES = 4
SWEEPS = 2
HALO = 16

huber_delta = 0.5
sweep_rate = 0.2

bf16 = jnp.bfloat16
f32 = jnp.float32


SMALL = 4 << 20

MASK = 0
HELD = 8
PICK = 40
FROM = 72
SCALE = 76
BOUND = 77
TABLE = 80

VMEM = pl.BlockSpec(memory_space=pltpu.VMEM)
SMEM = pl.BlockSpec(memory_space=pltpu.SMEM)
HBM = pl.BlockSpec(memory_space=pltpu.HBM)


def keep(x):
    return pltpu.with_memory_space_constraint(x, pltpu.HBM)


def prepare_kernel(step_gain, slabs, vol_hbm, meas_hbm, start_hbm, len_hbm, slot_hbm, relax_ref,
                   low_ref, high_ref, meas_ref, table_ref,
                   first, last, start_ref, len_ref, slot_ref, sem):
    rows, cells = vol_hbm.shape
    det = meas_ref.shape[1]
    tile = first.shape[0]
    pairs = [
        (vol_hbm.at[0:tile], first),
        (vol_hbm.at[rows - tile : rows], last),
        (meas_hbm, meas_ref),
        (start_hbm, start_ref),
        (len_hbm, len_ref),
        (slot_hbm, slot_ref),
    ]
    copies = [pltpu.make_async_copy(*pair, sem.at[i]) for i, pair in enumerate(pairs)]
    for copy in copies:
        copy.start()
    for copy in copies:
        copy.wait()
    orient = lax.axis_index("orient")
    slab = lax.axis_index("slab")
    lanes = lax.broadcasted_iota(jnp.int32, (1, det), 1)

    def line(flag):
        return jnp.full((1, det), jnp.where(flag, 1.0, 0.0), f32)

    for k in range(8):
        begin = start_ref[k]
        inside = (lanes >= begin) & (lanes < begin + len_ref[k])
        table_ref[MASK + k : MASK + k + 1, :] = jnp.where(inside, 1.0, 0.0)
    for s in range(FRAMES):
        image = slot_ref[jnp.bitwise_xor(orient, s)]
        refl = jnp.right_shift(image, 2)
        for k in range(8):
            wanted = k * FRAMES + jnp.bitwise_and(orient + k, FRAMES - 1)
            table_ref[HELD + 8 * s + k : HELD + 8 * s + k + 1, :] = line(image == wanted)
            table_ref[PICK + 8 * s + k : PICK + 8 * s + k + 1, :] = line(refl == k)
    mine = slot_ref[orient]
    source = jnp.bitwise_and(jnp.bitwise_xor(mine - jnp.right_shift(mine, 2), orient), FRAMES - 1)
    for s in range(FRAMES):
        table_ref[FROM + s : FROM + s + 1, :] = line(source == s)
    table_ref[SCALE : SCALE + 1, :] = jnp.full((1, det), relax_ref[0] * step_gain, f32)
    table_ref[BOUND : BOUND + 1, :] = line(slab != slabs - 1) * huber_delta
    table_ref[BOUND + 1 : BOUND + 2, :] = line(slab != 0) * huber_delta
    table_ref[BOUND + 2 : BOUND + 3, :] = line(slab < 0)
    low_ref[:, cells:] = meas_ref[rows - 2 :, :].astype(bf16)
    high_ref[:, cells:] = meas_ref[0:2, :].astype(bf16)
    high_ref[:, 0:cells] = first[0:2, :]
    low_ref[:, 0:cells] = last[tile - 2 :, :]


def prepare(vol, start, length, slot_image, meas, relax, step_gain, slabs):
    rows, cells = vol.shape
    det = meas.shape[1]
    edge = jax.ShapeDtypeStruct((2, cells + det), bf16)
    return pl.pallas_call(
        lambda *refs: prepare_kernel(step_gain, slabs, *refs),
        in_specs=[HBM] * 5 + [SMEM],
        out_specs=(VMEM,) * 4,
        out_shape=(
            edge, edge, jax.ShapeDtypeStruct(meas.shape, f32), jax.ShapeDtypeStruct((TABLE, det), f32)
        ),
        scratch_shapes=[
            pltpu.VMEM((HALO, cells), bf16),
            pltpu.VMEM((HALO, cells), bf16),
            pltpu.SMEM(start.shape, jnp.int32),
            pltpu.SMEM(length.shape, jnp.int32),
            pltpu.SMEM(slot_image.shape, jnp.int32),
            pltpu.SemaphoreType.DMA((6,)),
        ],
        compiler_params=pltpu.CompilerParams(vmem_limit_bytes=SMALL),
        name="prepare",
    )(*(keep(x) for x in (vol, meas, start, length, slot_image)), relax)


def extend_kernel(meas_ref, below_ref, above_ref, ext_ref):
    rows, det = meas_ref.shape
    cells = below_ref.shape[1] - det
    ext_ref[0:rows] = meas_ref[...].astype(bf16)
    ext_ref[rows:] = jnp.concatenate(
        [below_ref[:, cells:], jnp.zeros((HALO - 4, det), bf16), above_ref[:, cells:]], axis=0
    )


def extend(meas, below, above):
    rows, det = meas.shape
    return pl.pallas_call(
        extend_kernel,
        in_specs=[VMEM] * 3,
        out_specs=VMEM,
        out_shape=jax.ShapeDtypeStruct((rows + HALO, det), bf16),
        compiler_params=pltpu.CompilerParams(vmem_limit_bytes=SMALL),
        name="extend",
    )(meas, below, above)


def project_kernel(vol_hbm, below_ref, above_ref, rays_hbm, table_ref, proj_ref, flat_ref, vol_ref, buf, acc, vsem, rsem):
    chunks = rsem.shape[0]
    chunk = buf.shape[0] // chunks
    rows, cells = vol_hbm.shape
    refl, det = rays_hbm.shape[1:]

    def rays_copy(i):
        at = pl.ds(pl.multiple_of(i * chunk, chunk), chunk)
        return pltpu.make_async_copy(rays_hbm.at[at], buf.at[at], rsem.at[i])

    def vol_copy(i):
        at = pl.ds(pl.multiple_of(i * chunk, chunk), chunk)
        return pltpu.make_async_copy(vol_hbm.at[:, at], vol_ref.at[0:rows, at], vsem.at[i])

    for i in range(chunks):
        vol_copy(i).start()
        rays_copy(i).start()
    vol_ref[rows:, :] = jnp.concatenate(
        [below_ref[:, 0:cells], jnp.zeros((HALO - 4, cells), bf16), above_ref[:, 0:cells]], axis=0
    )
    acc[...] = jnp.zeros_like(acc)

    def step(i, carry):
        at = pl.ds(pl.multiple_of(i * chunk, chunk), chunk)
        vol_copy(i).wait()
        rays_copy(i).wait()
        flat = buf[at].reshape(chunk, refl * det)
        flat_ref[at, :] = flat
        acc[...] += jnp.dot(vol_ref[:, at], flat, preferred_element_type=f32)
        return carry

    lax.fori_loop(0, chunks, step, 0)
    for k in range(refl):
        proj_ref[k] = acc[:, k * det : (k + 1) * det] * table_ref[MASK + k : MASK + k + 1, :]


def project(vol, below, above, rays, table, chunk=1024):
    rows, cells = vol.shape
    refl, det = rays.shape[1:]
    ext = rows + HALO
    return pl.pallas_call(
        project_kernel,
        in_specs=[HBM, VMEM, VMEM, HBM, VMEM],
        out_specs=(VMEM, VMEM, VMEM),
        out_shape=(
            jax.ShapeDtypeStruct((refl, ext, det), f32),
            pltpu.VMEM((cells, refl * det), bf16),
            pltpu.VMEM((ext, cells), bf16),
        ),
        scratch_shapes=[
            pltpu.VMEM(rays.shape, bf16),
            pltpu.VMEM((ext, refl * det), f32),
            pltpu.SemaphoreType.DMA((cells // chunk,)),
            pltpu.SemaphoreType.DMA((cells // chunk,)),
        ],
        compiler_params=pltpu.CompilerParams(vmem_limit_bytes=24 << 20),
        name="project",
    )(keep(vol), below, above, keep(rays), table)


def combine_kernel(proj_ref, table_ref, *refs):
    gathered, part_ref = refs[:FRAMES], refs[FRAMES]
    images = [ref[...].astype(f32) for ref in gathered]
    for k in range(proj_ref.shape[0]):
        part = proj_ref[k]
        for s in range(FRAMES):
            row = HELD + 8 * s + k
            part = part - table_ref[row : row + 1, :] * images[s]
        part_ref[k] = part.astype(bf16)


def combine(proj, table, gathered):
    return pl.pallas_call(
        combine_kernel,
        in_specs=[VMEM] * (2 + FRAMES),
        out_specs=VMEM,
        out_shape=jax.ShapeDtypeStruct(proj.shape, bf16),
        compiler_params=pltpu.CompilerParams(vmem_limit_bytes=SMALL),
        name="combine",
    )(proj, table, *gathered)


def total_kernel(pieces_ref, out_ref):
    count = pieces_ref.shape[0]
    total = pieces_ref[0].astype(f32)
    for i in range(1, count):
        total = total + pieces_ref[i].astype(f32)
    own = (-total).astype(bf16)
    for i in range(count):
        out_ref[i] = own


def total(pieces):
    return pl.pallas_call(
        total_kernel,
        in_specs=[VMEM],
        out_specs=VMEM,
        out_shape=jax.ShapeDtypeStruct(pieces.shape, bf16),
        compiler_params=pltpu.CompilerParams(vmem_limit_bytes=SMALL),
        name="total",
    )(pieces)


def pick_kernel(img_ref, table_ref, *outs):
    rows = outs[0].shape[0]
    for s in range(FRAMES):
        image = jnp.zeros(outs[0].shape, f32)
        for k in range(img_ref.shape[0]):
            row = PICK + 8 * s + k
            image = image + table_ref[row : row + 1, :] * img_ref[k, 0:rows, :].astype(f32)
        outs[s][...] = image.astype(bf16)


def pick(img, table, rows):
    shape = jax.ShapeDtypeStruct((rows, img.shape[2]), bf16)
    return pl.pallas_call(
        pick_kernel,
        in_specs=[VMEM, VMEM],
        out_specs=(VMEM,) * FRAMES,
        out_shape=(shape,) * FRAMES,
        compiler_params=pltpu.CompilerParams(vmem_limit_bytes=SMALL),
        name="pick",
    )(img, table)


def choose_kernel(table_ref, *refs):
    image = jnp.zeros(refs[0].shape, f32)
    for s in range(FRAMES):
        image = image + table_ref[FROM + s : FROM + s + 1, :] * refs[s][...].astype(f32)
    refs[FRAMES][...] = image


def choose(table, images):
    return pl.pallas_call(
        choose_kernel,
        in_specs=[VMEM] * (1 + FRAMES),
        out_specs=VMEM,
        out_shape=jax.ShapeDtypeStruct(images[0].shape, f32),
        compiler_params=pltpu.CompilerParams(vmem_limit_bytes=SMALL),
        name="choose",
    )(table, *images)


def update_kernel(img_ref, table_ref, flat_ref, vol_ref, out_hbm, obuf, osem):
    refl = img_ref.shape[0]
    ext, cells = vol_ref.shape
    rows, chunk = obuf.shape[1:]
    img = jnp.concatenate(
        [img_ref[k] * table_ref[MASK + k : MASK + k + 1, :].astype(bf16) for k in range(refl)], axis=1
    )
    scale = table_ref[SCALE : SCALE + 1, 0:1]
    place = lax.broadcasted_iota(jnp.int32, (ext, 1), 0)
    bound = jnp.where(
        place == rows - 1,
        table_ref[BOUND : BOUND + 1, 0:1],
        jnp.where(place == ext - 1, table_ref[BOUND + 1 : BOUND + 2, 0:1], huber_delta),
    )

    def out_copy(i, slot):
        at = pl.ds(pl.multiple_of(i * chunk, chunk), chunk)
        return pltpu.make_async_copy(obuf.at[slot], out_hbm.at[:, at], osem.at[slot])

    def step(i, carry):
        at = pl.ds(pl.multiple_of(i * chunk, chunk), chunk)
        slot = lax.rem(i, 2)
        gradient = lax.dot_general(
            img, flat_ref[at, :], (((1,), (1,)), ((), ())), preferred_element_type=f32
        )
        density = vol_ref[:, at].astype(f32) + scale * gradient
        for _ in range(SWEEPS):
            flux = pltpu.roll(density, ext - 1, 0) - density
            flux = jnp.minimum(jnp.maximum(flux, -bound), bound)
            density = density + sweep_rate * (flux - pltpu.roll(flux, 1, 0))

        @pl.when(i >= 2)
        def _():
            out_copy(i - 2, slot).wait()

        obuf[slot] = density[:rows].astype(bf16)
        out_copy(i, slot).start()
        return carry

    steps = cells // chunk
    lax.fori_loop(0, steps, step, 0)
    for i in range(steps - 2, steps):
        out_copy(i, i % 2).wait()


def update(img, table, flat, vol_ext, chunk=1024):
    ext, cells = vol_ext.shape
    rows = ext - HALO
    return pl.pallas_call(
        update_kernel,
        in_specs=[VMEM] * 4,
        out_specs=HBM,
        out_shape=jax.ShapeDtypeStruct((rows, cells), bf16),
        scratch_shapes=[pltpu.VMEM((2, rows, chunk), bf16), pltpu.SemaphoreType.DMA((2,))],
        compiler_params=pltpu.CompilerParams(vmem_limit_bytes=24 << 20),
        name="update",
    )(img, table, flat, vol_ext)


def local(volume, rays, band_start, band_len, slot_image, measured, relax):
    cells, refl, det = rays.shape
    rows = volume.shape[1]
    slabs = lax.axis_size("slab")
    orients = lax.axis_size("orient")
    members = orients // FRAMES
    classes = [[g * FRAMES + q for g in range(members)] for q in range(FRAMES)]
    vol = volume[0]
    meas = measured[0]
    step_gain = math.sqrt(cells * orients / (FRAMES * refl * det))

    low, high, meas, table = prepare(
        vol, band_start[:, 0], band_len[:, 0], slot_image, meas, relax, step_gain, slabs
    )

    above = lax.ppermute(low, "slab", [(i, i + 1) for i in range(slabs - 1)])
    below = lax.ppermute(high, "slab", [(i + 1, i) for i in range(slabs - 1)])
    meas_ext = extend(meas, below, above)

    swaps = [[(o, o ^ s) for o in range(orients)] for s in range(FRAMES)]
    gathered = [meas_ext] + [lax.ppermute(meas_ext, "orient", swaps[s]) for s in range(1, FRAMES)]

    proj, flat, vol_ext = project(vol, below, above, rays, table)

    part = combine(proj, table, gathered)
    pieces = lax.all_to_all(part, "orient", 0, 0, axis_index_groups=classes, tiled=True)
    images = lax.all_to_all(total(pieces), "orient", 0, 0, axis_index_groups=classes, tiled=True)

    picked = pick(images, table, rows)
    arrived = [picked[0]] + [lax.ppermute(picked[s], "orient", swaps[s]) for s in range(1, FRAMES)]
    updated = update(images, table, flat, vol_ext)
    residual = choose(table, arrived)
    return (updated[None], residual[None])


def solution(mesh):
    placed = (
        P("orient", "slab", None),
        P(),
        P(None, "orient"),
        P(None, "orient"),
        P(),
        P("orient", "slab", None),
        P("orient"),
    )
    return jax.shard_map(
        local,
        mesh=mesh,
        in_specs=placed,
        out_specs=(P("orient", "slab", None), P("orient", "slab", None)),
        check_vma=False,
    )
```

```python
import math

import jax
import jax.numpy as jnp
from jax import lax
from jax.experimental import pallas as pl
from jax.experimental.pallas import tpu as pltpu
from jax.sharding import PartitionSpec as P

FRAMES = 4
SWEEPS = 2
HALO = 16

huber_delta = 0.5
sweep_rate = 0.2

bf16 = jnp.bfloat16
f32 = jnp.float32


PIECE = 64
SMALL = 4 << 20

MASK = 0
HELD = 8
PICK = 40
FROM = 72
SCALE = 76
BOUND = 77
TABLE = 80

VMEM = pl.BlockSpec(memory_space=pltpu.VMEM)
SMEM = pl.BlockSpec(memory_space=pltpu.SMEM)
HBM = pl.BlockSpec(memory_space=pltpu.HBM)


def keep(x):
    return pltpu.with_memory_space_constraint(x, pltpu.HBM)


def prepare_kernel(step_gain, slabs, vol_hbm, meas_hbm, start_hbm, len_hbm, slot_hbm, relax_ref,
                   near_ref, far_ref, meas_ref, table_ref,
                   first, last, start_ref, len_ref, slot_ref, sem):
    rows, cells = vol_hbm.shape
    det = meas_ref.shape[1]
    tile = first.shape[0]
    pairs = [
        (vol_hbm.at[0:tile], first),
        (vol_hbm.at[rows - tile : rows], last),
        (meas_hbm, meas_ref),
        (start_hbm, start_ref),
        (len_hbm, len_ref),
        (slot_hbm, slot_ref),
    ]
    copies = [pltpu.make_async_copy(*pair, sem.at[i]) for i, pair in enumerate(pairs)]
    for copy in copies:
        copy.start()
    for copy in copies:
        copy.wait()
    orient = lax.axis_index("orient")
    slab = lax.axis_index("slab")
    lanes = lax.broadcasted_iota(jnp.int32, (1, det), 1)

    def line(flag):
        return jnp.full((1, det), jnp.where(flag, 1.0, 0.0), f32)

    for k in range(8):
        begin = start_ref[k]
        inside = (lanes >= begin) & (lanes < begin + len_ref[k])
        table_ref[MASK + k : MASK + k + 1, :] = jnp.where(inside, 1.0, 0.0)
    for s in range(FRAMES):
        image = slot_ref[jnp.bitwise_xor(orient, s)]
        refl = jnp.right_shift(image, 2)
        for k in range(8):
            wanted = k * FRAMES + jnp.bitwise_and(orient + k, FRAMES - 1)
            table_ref[HELD + 8 * s + k : HELD + 8 * s + k + 1, :] = line(image == wanted)
            table_ref[PICK + 8 * s + k : PICK + 8 * s + k + 1, :] = line(refl == k)
    mine = slot_ref[orient]
    source = jnp.bitwise_and(jnp.bitwise_xor(mine - jnp.right_shift(mine, 2), orient), FRAMES - 1)
    for s in range(FRAMES):
        table_ref[FROM + s : FROM + s + 1, :] = line(source == s)
    table_ref[SCALE : SCALE + 1, :] = jnp.full((1, det), relax_ref[0] * step_gain, f32)
    table_ref[BOUND : BOUND + 1, :] = line(slab != slabs - 1) * huber_delta
    table_ref[BOUND + 1 : BOUND + 2, :] = line(slab != 0) * huber_delta
    table_ref[BOUND + 2 : BOUND + 3, :] = line(slab < 0)
    low = jnp.concatenate([last[tile - 2 :, :], meas_ref[rows - 2 :, :].astype(bf16)], axis=1)
    high = jnp.concatenate([first[0:2, :], meas_ref[0:2, :].astype(bf16)], axis=1)
    even = jnp.bitwise_and(slab, 1) == 0

    @pl.when(even)
    def _():
        near_ref[...] = low
        far_ref[...] = high

    @pl.when(jnp.logical_not(even))
    def _():
        near_ref[...] = high
        far_ref[...] = low


def prepare(vol, start, length, slot_image, meas, relax, step_gain, slabs):
    rows, cells = vol.shape
    det = meas.shape[1]
    edge = jax.ShapeDtypeStruct((2, cells + det), bf16)
    return pl.pallas_call(
        lambda *refs: prepare_kernel(step_gain, slabs, *refs),
        in_specs=[HBM] * 5 + [SMEM],
        out_specs=(VMEM,) * 4,
        out_shape=(
            edge, edge, jax.ShapeDtypeStruct(meas.shape, f32), jax.ShapeDtypeStruct((TABLE, det), f32)
        ),
        scratch_shapes=[
            pltpu.VMEM((HALO, cells), bf16),
            pltpu.VMEM((HALO, cells), bf16),
            pltpu.SMEM(start.shape, jnp.int32),
            pltpu.SMEM(length.shape, jnp.int32),
            pltpu.SMEM(slot_image.shape, jnp.int32),
            pltpu.SemaphoreType.DMA((6,)),
        ],
        compiler_params=pltpu.CompilerParams(vmem_limit_bytes=SMALL),
        name="prepare",
    )(*(keep(x) for x in (vol, meas, start, length, slot_image)), relax)


def halo_rows(near, far, even):
    below = jnp.where(even, near, far)
    above = jnp.where(even, far, near)
    zeros = jnp.zeros((HALO - 4, near.shape[1]), bf16)
    return jnp.concatenate([below, zeros, above], axis=0)


def extend_kernel(meas_ref, near_ref, far_ref, ext_ref):
    rows, det = meas_ref.shape
    cells = near_ref.shape[1] - det
    even = jnp.bitwise_and(lax.axis_index("slab"), 1) == 0
    ext_ref[0:rows] = meas_ref[...].astype(bf16)
    ext_ref[rows:] = halo_rows(near_ref[:, cells:], far_ref[:, cells:], even)


def extend(meas, near, far):
    rows, det = meas.shape
    return pl.pallas_call(
        extend_kernel,
        in_specs=[VMEM] * 3,
        out_specs=VMEM,
        out_shape=jax.ShapeDtypeStruct((rows + HALO, det), bf16),
        compiler_params=pltpu.CompilerParams(vmem_limit_bytes=SMALL),
        name="extend",
    )(meas, near, far)


def project_kernel(vol_hbm, near_ref, far_ref, rays_hbm, table_ref, proj_ref, flat_ref, vol_ref, buf, acc, vsem, rsem):
    chunks = rsem.shape[0]
    rows, cells = vol_hbm.shape
    chunk = cells // chunks
    refl = buf.shape[0] // cells
    det = buf.shape[1]

    def copies(i):
        at = slice(i * chunk, (i + 1) * chunk)
        wide = slice(i * chunk * refl, (i + 1) * chunk * refl)
        return (
            pltpu.make_async_copy(vol_hbm.at[:, at], vol_ref.at[0:rows, at], vsem.at[i]),
            pltpu.make_async_copy(rays_hbm.at[wide], buf.at[wide], rsem.at[i]),
        )

    for i in range(chunks):
        for copy in copies(i):
            copy.start()
    even = jnp.bitwise_and(lax.axis_index("slab"), 1) == 0
    vol_ref[rows:, :] = halo_rows(near_ref[:, 0:cells], far_ref[:, 0:cells], even)
    for i in range(chunks):
        for copy in copies(i):
            copy.wait()
        at = slice(i * chunk, (i + 1) * chunk)
        for j in range(i * chunk, (i + 1) * chunk, PIECE):
            flat_ref[j : j + PIECE, :] = buf[j * refl : (j + PIECE) * refl].reshape(PIECE, refl * det)
        part = jnp.dot(vol_ref[:, at], flat_ref[at, :], preferred_element_type=f32)
        acc[...] = part if i == 0 else acc[...] + part
    for k in range(refl):
        proj_ref[k] = acc[:, k * det : (k + 1) * det] * table_ref[MASK + k : MASK + k + 1, :]


def project(vol, near, far, rays, table, chunk=1024):
    rows, cells = vol.shape
    refl, det = rays.shape[1:]
    ext = rows + HALO
    return pl.pallas_call(
        project_kernel,
        in_specs=[HBM, VMEM, VMEM, HBM, VMEM],
        out_specs=(VMEM, VMEM, VMEM),
        out_shape=(
            jax.ShapeDtypeStruct((refl, ext, det), f32),
            pltpu.VMEM((cells, refl * det), bf16),
            pltpu.VMEM((ext, cells), bf16),
        ),
        scratch_shapes=[
            pltpu.VMEM((cells * refl, det), bf16),
            pltpu.VMEM((ext, refl * det), f32),
            pltpu.SemaphoreType.DMA((cells // chunk,)),
            pltpu.SemaphoreType.DMA((cells // chunk,)),
        ],
        compiler_params=pltpu.CompilerParams(vmem_limit_bytes=24 << 20),
        name="project",
    )(keep(vol), near, far, keep(rays.reshape(cells * refl, det)), table)


def fold_kernel(flat_ref, table_ref, out_ref):
    cells, wide = flat_ref.shape
    det = table_ref.shape[1]
    low = lax.broadcasted_iota(jnp.int32, (1, det), 1) < det // 2
    low_block = jnp.broadcast_to(low, (PIECE, det))
    keeps = []
    for p in range(wide // (2 * det)):
        k = MASK + 2 * p
        line = jnp.where(low, table_ref[k : k + 1, :], table_ref[k + 1 : k + 2, :])
        keeps.append(jnp.broadcast_to(line.astype(bf16), (PIECE, det)) > 0.5)

    def step(i, carry):
        at = pl.ds(pl.multiple_of(i * PIECE, PIECE), PIECE)
        for p, stay in enumerate(keeps):
            first = flat_ref[at, 2 * p * det : (2 * p + 1) * det]
            second = flat_ref[at, (2 * p + 1) * det : (2 * p + 2) * det]
            straight = jnp.where(low_block, first, second)
            crossed = jnp.where(low_block, second, first)
            out_ref[at, p * det : (p + 1) * det] = jnp.where(
                stay, straight, pltpu.roll(crossed, det // 2, 1)
            )
        return carry

    lax.fori_loop(0, cells // PIECE, step, 0)


def fold(flat, table):
    cells, wide = flat.shape
    return pl.pallas_call(
        fold_kernel,
        in_specs=[VMEM, VMEM],
        out_specs=VMEM,
        out_shape=pltpu.VMEM((cells, wide // 2), bf16),
        compiler_params=pltpu.CompilerParams(vmem_limit_bytes=SMALL),
        name="fold",
    )(flat, table)


def combine_kernel(proj_ref, table_ref, *refs):
    gathered, part_ref = refs[:FRAMES], refs[FRAMES]
    images = [ref[...].astype(f32) for ref in gathered]
    for k in range(proj_ref.shape[0]):
        part = proj_ref[k]
        for s in range(FRAMES):
            row = HELD + 8 * s + k
            part = part - table_ref[row : row + 1, :] * images[s]
        part_ref[k] = part.astype(bf16)


def combine(proj, table, gathered):
    return pl.pallas_call(
        combine_kernel,
        in_specs=[VMEM] * (2 + FRAMES),
        out_specs=VMEM,
        out_shape=jax.ShapeDtypeStruct(proj.shape, bf16),
        compiler_params=pltpu.CompilerParams(vmem_limit_bytes=SMALL),
        name="combine",
    )(proj, table, *gathered)


def total_kernel(pieces_ref, out_ref):
    count = pieces_ref.shape[0]
    total = pieces_ref[0].astype(f32)
    for i in range(1, count):
        total = total + pieces_ref[i].astype(f32)
    own = (-total).astype(bf16)
    for i in range(count):
        out_ref[i] = own


def total(pieces):
    return pl.pallas_call(
        total_kernel,
        in_specs=[VMEM],
        out_specs=VMEM,
        out_shape=jax.ShapeDtypeStruct(pieces.shape, bf16),
        compiler_params=pltpu.CompilerParams(vmem_limit_bytes=SMALL),
        name="total",
    )(pieces)


def pick_kernel(img_ref, table_ref, *outs):
    rows = outs[0].shape[0]
    for s in range(FRAMES):
        image = jnp.zeros(outs[0].shape, f32)
        for k in range(img_ref.shape[0]):
            row = PICK + 8 * s + k
            image = image + table_ref[row : row + 1, :] * img_ref[k, 0:rows, :].astype(f32)
        outs[s][...] = image.astype(bf16)


def pick(img, table, rows):
    shape = jax.ShapeDtypeStruct((rows, img.shape[2]), bf16)
    return pl.pallas_call(
        pick_kernel,
        in_specs=[VMEM, VMEM],
        out_specs=(VMEM,) * FRAMES,
        out_shape=(shape,) * FRAMES,
        compiler_params=pltpu.CompilerParams(vmem_limit_bytes=SMALL),
        name="pick",
    )(img, table)


def choose_kernel(table_ref, *refs):
    image = jnp.zeros(refs[0].shape, f32)
    for s in range(FRAMES):
        image = image + table_ref[FROM + s : FROM + s + 1, :] * refs[s][...].astype(f32)
    refs[FRAMES][...] = image


def choose(table, images):
    return pl.pallas_call(
        choose_kernel,
        in_specs=[VMEM] * (1 + FRAMES),
        out_specs=VMEM,
        out_shape=jax.ShapeDtypeStruct(images[0].shape, f32),
        compiler_params=pltpu.CompilerParams(vmem_limit_bytes=SMALL),
        name="choose",
    )(table, *images)


def update_kernel(img_ref, table_ref, flat_ref, vol_ref, out_hbm, dbuf, fbuf, obuf, osem):
    refl, ext, det = img_ref.shape
    cells = vol_ref.shape[1]
    rows = ext - HALO
    slots = dbuf.shape[0]
    tiles = slots // 2
    chunk = tiles * det
    steps = cells // chunk
    sends = osem.shape[0]

    low = lax.broadcasted_iota(jnp.int32, (1, det), 1) < det // 2
    parts = []
    for k in range(0, refl, 2):
        first = img_ref[k].astype(f32) * table_ref[MASK + k : MASK + k + 1, :]
        second = img_ref[k + 1].astype(f32) * table_ref[MASK + k + 1 : MASK + k + 2, :]
        straight = jnp.where(low, first, second)
        crossed = jnp.where(low, second, first)
        parts.append((straight + pltpu.roll(crossed, det // 2, 1)).astype(bf16))
    img = jnp.concatenate(parts, axis=1)
    scale = table_ref[SCALE : SCALE + 1, 0:1]

    place = lax.broadcasted_iota(jnp.int32, (ext, det), 0)
    bound = jnp.where(
        place == rows + 7,
        table_ref[BOUND : BOUND + 1, :],
        jnp.where(place == 7, table_ref[BOUND + 1 : BOUND + 2, :], huber_delta),
    )
    zeros = jnp.zeros((8, det), f32)
    for q in range(slots):
        dbuf[q, 0:8] = zeros
        dbuf[q, 8 + ext :] = zeros
        fbuf[q, 0:8] = zeros

    def psi(t, first):
        limit = bound[first : first + t.shape[0]]
        return jnp.minimum(jnp.maximum(t, -limit), limit)

    def backproject(i):
        at = slice(i * chunk, (i + 1) * chunk)
        gradient = lax.dot_general(
            img, flat_ref[at, :], (((1,), (1,)), ((), ())), preferred_element_type=f32
        )
        density = vol_ref[:, at].astype(f32) + scale * gradient
        for t in range(tiles):
            q = (i * tiles + t) % slots
            lanes = slice(t * det, (t + 1) * det)
            dbuf[q, 8:16] = density[ext - 8 :, lanes]
            dbuf[q, 16 : 8 + ext] = density[0 : ext - 8, lanes]

    def out_copy(j):
        at = slice(j * (cells // sends), (j + 1) * (cells // sends))
        return pltpu.make_async_copy(obuf.at[:, at], out_hbm.at[:, at], osem.at[j])

    def smooth(i):
        for t in range(tiles):
            q = (i * tiles + t) % slots
            here = dbuf[q, 8 : 8 + ext]
            flux = psi(dbuf[q, 9 : 9 + ext] - here, 0)
            fbuf[q, 8 : 8 + ext] = flux
            once = here + sweep_rate * (flux - fbuf[q, 7 : 7 + ext])
            dbuf[q, 8 : 8 + ext] = once
            fbuf[q, 8 : 16 + rows] = psi(dbuf[q, 9 : 17 + rows] - once[0 : 8 + rows], 0)
            net = fbuf[q, 16 : 16 + rows] - fbuf[q, 15 : 15 + rows]
            at = slice(i * chunk + t * det, i * chunk + (t + 1) * det)
            obuf[:, at] = (once[8 : 8 + rows] + sweep_rate * net).astype(bf16)
        if (i + 1) * sends % steps == 0:
            out_copy((i + 1) * sends // steps - 1).start()

    backproject(0)
    for i in range(1, steps):
        backproject(i)
        smooth(i - 1)
    smooth(steps - 1)
    for j in range(sends):
        out_copy(j).wait()


def update(img, table, flat, vol_ext, chunk=256, sends=8):
    ext, cells = vol_ext.shape
    rows = ext - HALO
    det = img.shape[2]
    slot = pltpu.VMEM((2 * chunk // det, ext + 16, det), f32)
    return pl.pallas_call(
        update_kernel,
        in_specs=[VMEM] * 4,
        out_specs=HBM,
        out_shape=jax.ShapeDtypeStruct((rows, cells), bf16),
        scratch_shapes=[slot, slot, pltpu.VMEM((rows, cells), bf16), pltpu.SemaphoreType.DMA((sends,))],
        compiler_params=pltpu.CompilerParams(vmem_limit_bytes=8 << 20),
        name="update",
    )(img, table, flat, vol_ext)


def local(volume, rays, band_start, band_len, slot_image, measured, relax):
    cells, refl, det = rays.shape
    rows = volume.shape[1]
    slabs = lax.axis_size("slab")
    orients = lax.axis_size("orient")
    members = orients // FRAMES
    classes = [[g * FRAMES + q for g in range(members)] for q in range(FRAMES)]
    vol = volume[0]
    meas = measured[0]
    step_gain = math.sqrt(cells * orients / (FRAMES * refl * det))

    near, far, meas, table = prepare(
        vol, band_start[:, 0], band_len[:, 0], slot_image, meas, relax, step_gain, slabs
    )

    near = lax.ppermute(near, "slab", [(i, i ^ 1) for i in range(slabs)])
    far = lax.ppermute(far, "slab", [(i, slabs - 1 - i) for i in range(slabs)])
    meas_ext = extend(meas, near, far)

    swaps = [[(o, o ^ s) for o in range(orients)] for s in range(FRAMES)]
    gathered = [meas_ext] + [lax.ppermute(meas_ext, "orient", swaps[s]) for s in range(1, FRAMES)]

    proj, flat, vol_ext = project(vol, near, far, rays, table)
    flat = fold(flat, table)

    part = combine(proj, table, gathered)
    pieces = lax.all_to_all(part, "orient", 0, 0, axis_index_groups=classes, tiled=True)
    images = lax.all_to_all(total(pieces), "orient", 0, 0, axis_index_groups=classes, tiled=True)

    picked = pick(images, table, rows)
    arrived = [picked[0]] + [lax.ppermute(picked[s], "orient", swaps[s]) for s in range(1, FRAMES)]
    updated = update(images, table, flat, vol_ext)
    residual = choose(table, arrived)
    return (updated[None], residual[None])


def solution(mesh):
    placed = (
        P("orient", "slab", None),
        P(),
        P(None, "orient"),
        P(None, "orient"),
        P(),
        P("orient", "slab", None),
        P("orient"),
    )
    return jax.shard_map(
        local,
        mesh=mesh,
        in_specs=placed,
        out_specs=(P("orient", "slab", None), P("orient", "slab", None)),
        check_vma=False,
    )
```

```python
import math

import jax
import jax.numpy as jnp
from jax import lax
from jax.experimental import pallas as pl
from jax.experimental.pallas import tpu as pltpu
from jax.sharding import PartitionSpec as P

FRAMES = 4
SWEEPS = 2
HALO = 16

huber_delta = 0.5
sweep_rate = 0.2

bf16 = jnp.bfloat16
f32 = jnp.float32


PIECE = 64
SMALL = 4 << 20

MASK = 0
HELD = 8
PICK = 40
FROM = 72
SCALE = 76
BOUND = 77
TABLE = 80

VMEM = pl.BlockSpec(memory_space=pltpu.VMEM)
SMEM = pl.BlockSpec(memory_space=pltpu.SMEM)
HBM = pl.BlockSpec(memory_space=pltpu.HBM)


def keep(x):
    return pltpu.with_memory_space_constraint(x, pltpu.HBM)


def prepare_kernel(step_gain, slabs, vol_hbm, meas_hbm, start_hbm, len_hbm, slot_hbm, relax_ref,
                   near_ref, far_ref, meas_ref, table_ref,
                   first, last, start_ref, len_ref, slot_ref, sem):
    rows, cells = vol_hbm.shape
    det = meas_ref.shape[1]
    tile = first.shape[0]
    pairs = [
        (vol_hbm.at[0:tile], first),
        (vol_hbm.at[rows - tile : rows], last),
        (meas_hbm, meas_ref),
        (start_hbm, start_ref),
        (len_hbm, len_ref),
        (slot_hbm, slot_ref),
    ]
    copies = [pltpu.make_async_copy(*pair, sem.at[i]) for i, pair in enumerate(pairs)]
    for copy in copies:
        copy.start()
    for copy in copies:
        copy.wait()
    orient = lax.axis_index("orient")
    slab = lax.axis_index("slab")
    lanes = lax.broadcasted_iota(jnp.int32, (1, det), 1)

    def line(flag):
        return jnp.full((1, det), jnp.where(flag, 1.0, 0.0), f32)

    for k in range(8):
        begin = start_ref[k]
        inside = (lanes >= begin) & (lanes < begin + len_ref[k])
        table_ref[MASK + k : MASK + k + 1, :] = jnp.where(inside, 1.0, 0.0)
    for s in range(FRAMES):
        image = slot_ref[jnp.bitwise_xor(orient, s)]
        refl = jnp.right_shift(image, 2)
        for k in range(8):
            wanted = k * FRAMES + jnp.bitwise_and(orient + k, FRAMES - 1)
            table_ref[HELD + 8 * s + k : HELD + 8 * s + k + 1, :] = line(image == wanted)
            table_ref[PICK + 8 * s + k : PICK + 8 * s + k + 1, :] = line(refl == k)
    mine = slot_ref[orient]
    source = jnp.bitwise_and(jnp.bitwise_xor(mine - jnp.right_shift(mine, 2), orient), FRAMES - 1)
    for s in range(FRAMES):
        table_ref[FROM + s : FROM + s + 1, :] = line(source == s)
    table_ref[SCALE : SCALE + 1, :] = jnp.full((1, det), relax_ref[0] * step_gain, f32)
    table_ref[BOUND : BOUND + 1, :] = line(slab != slabs - 1) * huber_delta
    table_ref[BOUND + 1 : BOUND + 2, :] = line(slab != 0) * huber_delta
    table_ref[BOUND + 2 : BOUND + 3, :] = line(slab < 0)
    low = jnp.concatenate([last[tile - 2 :, :], meas_ref[rows - 2 :, :].astype(bf16)], axis=1)
    high = jnp.concatenate([first[0:2, :], meas_ref[0:2, :].astype(bf16)], axis=1)
    even = jnp.bitwise_and(slab, 1) == 0

    @pl.when(even)
    def _():
        near_ref[...] = low
        far_ref[...] = high

    @pl.when(jnp.logical_not(even))
    def _():
        near_ref[...] = high
        far_ref[...] = low


def prepare(vol, start, length, slot_image, meas, relax, step_gain, slabs):
    rows, cells = vol.shape
    det = meas.shape[1]
    edge = jax.ShapeDtypeStruct((2, cells + det), bf16)
    return pl.pallas_call(
        lambda *refs: prepare_kernel(step_gain, slabs, *refs),
        in_specs=[HBM] * 5 + [SMEM],
        out_specs=(VMEM,) * 4,
        out_shape=(
            edge, edge, jax.ShapeDtypeStruct(meas.shape, f32), jax.ShapeDtypeStruct((TABLE, det), f32)
        ),
        scratch_shapes=[
            pltpu.VMEM((HALO, cells), bf16),
            pltpu.VMEM((HALO, cells), bf16),
            pltpu.SMEM(start.shape, jnp.int32),
            pltpu.SMEM(length.shape, jnp.int32),
            pltpu.SMEM(slot_image.shape, jnp.int32),
            pltpu.SemaphoreType.DMA((6,)),
        ],
        compiler_params=pltpu.CompilerParams(vmem_limit_bytes=SMALL),
        name="prepare",
    )(*(keep(x) for x in (vol, meas, start, length, slot_image)), relax)


def halo_rows(near, far, even):
    below = jnp.where(even, near, far)
    above = jnp.where(even, far, near)
    zeros = jnp.zeros((HALO - 4, near.shape[1]), bf16)
    return jnp.concatenate([below, zeros, above], axis=0)


def extend_kernel(meas_ref, near_ref, far_ref, ext_ref):
    rows, det = meas_ref.shape
    cells = near_ref.shape[1] - det
    even = jnp.bitwise_and(lax.axis_index("slab"), 1) == 0
    ext_ref[0:rows] = meas_ref[...].astype(bf16)
    ext_ref[rows:] = halo_rows(near_ref[:, cells:], far_ref[:, cells:], even)


def extend(meas, near, far):
    rows, det = meas.shape
    return pl.pallas_call(
        extend_kernel,
        in_specs=[VMEM] * 3,
        out_specs=VMEM,
        out_shape=jax.ShapeDtypeStruct((rows + HALO, det), bf16),
        compiler_params=pltpu.CompilerParams(vmem_limit_bytes=SMALL),
        name="extend",
    )(meas, near, far)


def project_kernel(vol_hbm, near_ref, far_ref, rays_hbm, table_ref, proj_ref, flat_ref, vol_ref, buf, acc, vsem, rsem):
    chunks = rsem.shape[0]
    rows, cells = vol_hbm.shape
    chunk = cells // chunks
    refl = buf.shape[0] // cells
    det = buf.shape[1]

    def copies(i):
        at = slice(i * chunk, (i + 1) * chunk)
        wide = slice(i * chunk * refl, (i + 1) * chunk * refl)
        return (
            pltpu.make_async_copy(vol_hbm.at[:, at], vol_ref.at[0:rows, at], vsem.at[i]),
            pltpu.make_async_copy(rays_hbm.at[wide], buf.at[wide], rsem.at[i]),
        )

    for i in range(chunks):
        for copy in copies(i):
            copy.start()
    even = jnp.bitwise_and(lax.axis_index("slab"), 1) == 0
    vol_ref[rows:, :] = halo_rows(near_ref[:, 0:cells], far_ref[:, 0:cells], even)
    for i in range(chunks):
        for copy in copies(i):
            copy.wait()
        at = slice(i * chunk, (i + 1) * chunk)
        for j in range(i * chunk, (i + 1) * chunk, PIECE):
            flat_ref[j : j + PIECE, :] = buf[j * refl : (j + PIECE) * refl].reshape(PIECE, refl * det)
        part = jnp.dot(vol_ref[:, at], flat_ref[at, :], preferred_element_type=f32)
        acc[...] = part if i == 0 else acc[...] + part
    for k in range(refl):
        proj_ref[k] = acc[:, k * det : (k + 1) * det] * table_ref[MASK + k : MASK + k + 1, :]


def project(vol, near, far, rays, table, chunk=1024):
    rows, cells = vol.shape
    refl, det = rays.shape[1:]
    ext = rows + HALO
    return pl.pallas_call(
        project_kernel,
        in_specs=[HBM, VMEM, VMEM, HBM, VMEM],
        out_specs=(VMEM, VMEM, VMEM),
        out_shape=(
            jax.ShapeDtypeStruct((refl, ext, det), f32),
            pltpu.VMEM((cells, refl * det), bf16),
            pltpu.VMEM((ext, cells), bf16),
        ),
        scratch_shapes=[
            pltpu.VMEM((cells * refl, det), bf16),
            pltpu.VMEM((ext, refl * det), f32),
            pltpu.SemaphoreType.DMA((cells // chunk,)),
            pltpu.SemaphoreType.DMA((cells // chunk,)),
        ],
        compiler_params=pltpu.CompilerParams(vmem_limit_bytes=24 << 20),
        name="project",
    )(keep(vol), near, far, keep(rays.reshape(cells * refl, det)), table)


def fold_kernel(flat_ref, table_ref, out_ref):
    cells, wide = flat_ref.shape
    det = table_ref.shape[1]
    block = 8 * PIECE
    low = lax.broadcasted_iota(jnp.int32, (1, det), 1) < det // 2
    low_block = jnp.broadcast_to(low, (block, det))
    keeps = []
    for p in range(wide // (2 * det)):
        k = MASK + 2 * p
        line = jnp.where(low, table_ref[k : k + 1, :], table_ref[k + 1 : k + 2, :])
        keeps.append(jnp.broadcast_to(line.astype(bf16), (block, det)) > 0.5)

    def step(i, carry):
        at = pl.ds(pl.multiple_of(i * block, block), block)
        for p, stay in enumerate(keeps):
            first = flat_ref[at, 2 * p * det : (2 * p + 1) * det]
            second = flat_ref[at, (2 * p + 1) * det : (2 * p + 2) * det]
            straight = jnp.where(low_block, first, second)
            crossed = jnp.where(low_block, second, first)
            out_ref[at, p * det : (p + 1) * det] = jnp.where(
                stay, straight, pltpu.roll(crossed, det // 2, 1)
            )
        return carry

    lax.fori_loop(0, cells // block, step, 0)


def fold(flat, table):
    cells, wide = flat.shape
    return pl.pallas_call(
        fold_kernel,
        in_specs=[VMEM, VMEM],
        out_specs=VMEM,
        out_shape=pltpu.VMEM((cells, wide // 2), bf16),
        compiler_params=pltpu.CompilerParams(vmem_limit_bytes=SMALL),
        name="fold",
    )(flat, table)


def combine_kernel(proj_ref, table_ref, *refs):
    gathered, part_ref = refs[:FRAMES], refs[FRAMES]
    images = [ref[...].astype(f32) for ref in gathered]
    for k in range(proj_ref.shape[0]):
        part = proj_ref[k]
        for s in range(FRAMES):
            row = HELD + 8 * s + k
            part = part - table_ref[row : row + 1, :] * images[s]
        part_ref[k] = part.astype(bf16)


def combine(proj, table, gathered):
    return pl.pallas_call(
        combine_kernel,
        in_specs=[VMEM] * (2 + FRAMES),
        out_specs=VMEM,
        out_shape=jax.ShapeDtypeStruct(proj.shape, bf16),
        compiler_params=pltpu.CompilerParams(vmem_limit_bytes=SMALL),
        name="combine",
    )(proj, table, *gathered)


def total_kernel(pieces_ref, out_ref):
    count = pieces_ref.shape[0]
    total = pieces_ref[0].astype(f32)
    for i in range(1, count):
        total = total + pieces_ref[i].astype(f32)
    own = (-total).astype(bf16)
    for i in range(count):
        out_ref[i] = own


def total(pieces):
    return pl.pallas_call(
        total_kernel,
        in_specs=[VMEM],
        out_specs=VMEM,
        out_shape=jax.ShapeDtypeStruct(pieces.shape, bf16),
        compiler_params=pltpu.CompilerParams(vmem_limit_bytes=SMALL),
        name="total",
    )(pieces)


def pick_kernel(img_ref, table_ref, *outs):
    rows = outs[0].shape[0]
    for s in range(FRAMES):
        image = jnp.zeros(outs[0].shape, f32)
        for k in range(img_ref.shape[0]):
            row = PICK + 8 * s + k
            image = image + table_ref[row : row + 1, :] * img_ref[k, 0:rows, :].astype(f32)
        outs[s][...] = image.astype(bf16)


def pick(img, table, rows):
    shape = jax.ShapeDtypeStruct((rows, img.shape[2]), bf16)
    return pl.pallas_call(
        pick_kernel,
        in_specs=[VMEM, VMEM],
        out_specs=(VMEM,) * FRAMES,
        out_shape=(shape,) * FRAMES,
        compiler_params=pltpu.CompilerParams(vmem_limit_bytes=SMALL),
        name="pick",
    )(img, table)


def choose_kernel(table_ref, *refs):
    image = jnp.zeros(refs[0].shape, f32)
    for s in range(FRAMES):
        image = image + table_ref[FROM + s : FROM + s + 1, :] * refs[s][...].astype(f32)
    refs[FRAMES][...] = image


def choose(table, images):
    return pl.pallas_call(
        choose_kernel,
        in_specs=[VMEM] * (1 + FRAMES),
        out_specs=VMEM,
        out_shape=jax.ShapeDtypeStruct(images[0].shape, f32),
        compiler_params=pltpu.CompilerParams(vmem_limit_bytes=SMALL),
        name="choose",
    )(table, *images)


def update_kernel(img_ref, table_ref, flat_ref, vol_ref, out_hbm, dbuf, fbuf, obuf, osem):
    refl, ext, det = img_ref.shape
    cells = vol_ref.shape[1]
    rows = ext - HALO
    slots = dbuf.shape[0]
    tiles = slots // 2
    chunk = tiles * det
    steps = cells // chunk
    sends = osem.shape[0]

    low = lax.broadcasted_iota(jnp.int32, (1, det), 1) < det // 2
    parts = []
    for k in range(0, refl, 2):
        first = img_ref[k].astype(f32) * table_ref[MASK + k : MASK + k + 1, :]
        second = img_ref[k + 1].astype(f32) * table_ref[MASK + k + 1 : MASK + k + 2, :]
        straight = jnp.where(low, first, second)
        crossed = jnp.where(low, second, first)
        parts.append((straight + pltpu.roll(crossed, det // 2, 1)).astype(bf16))
    img = jnp.concatenate(parts, axis=1)
    scale = table_ref[SCALE : SCALE + 1, 0:1]

    place = lax.broadcasted_iota(jnp.int32, (ext, det), 0)
    bound = jnp.where(
        place == rows + 7,
        table_ref[BOUND : BOUND + 1, :],
        jnp.where(place == 7, table_ref[BOUND + 1 : BOUND + 2, :], huber_delta),
    )
    zeros = jnp.zeros((8, det), f32)
    for q in range(slots):
        dbuf[q, 0:8] = zeros
        dbuf[q, 8 + ext :] = zeros
        fbuf[q, 0:8] = zeros

    def psi(t, first):
        limit = bound[first : first + t.shape[0]]
        return jnp.minimum(jnp.maximum(t, -limit), limit)

    def backproject(i):
        at = slice(i * chunk, (i + 1) * chunk)
        gradient = lax.dot_general(
            img, flat_ref[at, :], (((1,), (1,)), ((), ())), preferred_element_type=f32
        )
        density = vol_ref[:, at].astype(f32) + scale * gradient
        for t in range(tiles):
            q = (i * tiles + t) % slots
            lanes = slice(t * det, (t + 1) * det)
            dbuf[q, 8:16] = density[ext - 8 :, lanes]
            dbuf[q, 16 : 8 + ext] = density[0 : ext - 8, lanes]

    def out_copy(j):
        at = slice(j * (cells // sends), (j + 1) * (cells // sends))
        return pltpu.make_async_copy(obuf.at[:, at], out_hbm.at[:, at], osem.at[j])

    def smooth(i):
        for t in range(tiles):
            q = (i * tiles + t) % slots
            here = dbuf[q, 8 : 8 + ext]
            flux = psi(dbuf[q, 9 : 9 + ext] - here, 0)
            fbuf[q, 8 : 8 + ext] = flux
            once = here + sweep_rate * (flux - fbuf[q, 7 : 7 + ext])
            dbuf[q, 8 : 8 + ext] = once
            fbuf[q, 8 : 16 + rows] = psi(dbuf[q, 9 : 17 + rows] - once[0 : 8 + rows], 0)
            net = fbuf[q, 16 : 16 + rows] - fbuf[q, 15 : 15 + rows]
            at = slice(i * chunk + t * det, i * chunk + (t + 1) * det)
            obuf[:, at] = (once[8 : 8 + rows] + sweep_rate * net).astype(bf16)
        if (i + 1) * sends % steps == 0:
            out_copy((i + 1) * sends // steps - 1).start()

    backproject(0)
    for i in range(1, steps):
        backproject(i)
        smooth(i - 1)
    smooth(steps - 1)
    for j in range(sends):
        out_copy(j).wait()


def update(img, table, flat, vol_ext, chunk=256, sends=8):
    ext, cells = vol_ext.shape
    rows = ext - HALO
    det = img.shape[2]
    slot = pltpu.VMEM((2 * chunk // det, ext + 16, det), f32)
    return pl.pallas_call(
        update_kernel,
        in_specs=[VMEM] * 4,
        out_specs=HBM,
        out_shape=jax.ShapeDtypeStruct((rows, cells), bf16),
        scratch_shapes=[slot, slot, pltpu.VMEM((rows, cells), bf16), pltpu.SemaphoreType.DMA((sends,))],
        compiler_params=pltpu.CompilerParams(vmem_limit_bytes=8 << 20),
        name="update",
    )(img, table, flat, vol_ext)


def local(volume, rays, band_start, band_len, slot_image, measured, relax):
    cells, refl, det = rays.shape
    rows = volume.shape[1]
    slabs = lax.axis_size("slab")
    orients = lax.axis_size("orient")
    members = orients // FRAMES
    classes = [[g * FRAMES + q for g in range(members)] for q in range(FRAMES)]
    vol = volume[0]
    meas = measured[0]
    step_gain = math.sqrt(cells * orients / (FRAMES * refl * det))

    near, far, meas, table = prepare(
        vol, band_start[:, 0], band_len[:, 0], slot_image, meas, relax, step_gain, slabs
    )

    near = lax.ppermute(near, "slab", [(i, i ^ 1) for i in range(slabs)])
    far = lax.ppermute(far, "slab", [(i, slabs - 1 - i) for i in range(slabs)])
    meas_ext = extend(meas, near, far)

    swaps = [[(o, o ^ s) for o in range(orients)] for s in range(FRAMES)]
    gathered = [meas_ext] + [lax.ppermute(meas_ext, "orient", swaps[s]) for s in range(1, FRAMES)]

    proj, flat, vol_ext = project(vol, near, far, rays, table)
    flat = fold(flat, table)

    part = combine(proj, table, gathered)
    pieces = lax.all_to_all(part, "orient", 0, 0, axis_index_groups=classes, tiled=True)
    images = lax.all_to_all(total(pieces), "orient", 0, 0, axis_index_groups=classes, tiled=True)

    picked = pick(images, table, rows)
    arrived = [picked[0]] + [lax.ppermute(picked[s], "orient", swaps[s]) for s in range(1, FRAMES)]
    updated = update(images, table, flat, vol_ext)
    residual = choose(table, arrived)
    return (updated[None], residual[None])


def solution(mesh):
    placed = (
        P("orient", "slab", None),
        P(),
        P(None, "orient"),
        P(None, "orient"),
        P(),
        P("orient", "slab", None),
        P("orient"),
    )
    return jax.shard_map(
        local,
        mesh=mesh,
        in_specs=placed,
        out_specs=(P("orient", "slab", None), P("orient", "slab", None)),
        check_vma=False,
    )
```

```python
import math

import jax
import jax.numpy as jnp
from jax import lax
from jax.experimental import pallas as pl
from jax.experimental.pallas import tpu as pltpu
from jax.sharding import PartitionSpec as P

FRAMES = 4
SWEEPS = 2
HALO = 16

huber_delta = 0.5
sweep_rate = 0.2

bf16 = jnp.bfloat16
f32 = jnp.float32


CHUNKS = 8
SMALL = 4 << 20

MASK = 0
HELD = 8
PICK = 40
FROM = 72
SCALE = 76
BOUND = 77
TABLE = 80

VMEM = pl.BlockSpec(memory_space=pltpu.VMEM)
SMEM = pl.BlockSpec(memory_space=pltpu.SMEM)
HBM = pl.BlockSpec(memory_space=pltpu.HBM)


def keep(x):
    return pltpu.with_memory_space_constraint(x, pltpu.HBM)


def prepare_kernel(step_gain, slabs, vol_hbm, meas_hbm, start_hbm, len_hbm, slot_hbm, relax_ref,
                   near_ref, far_ref, meas_ref, table_ref,
                   first, last, start_ref, len_ref, slot_ref, sem):
    rows, cells = vol_hbm.shape
    det = meas_ref.shape[1]
    tile = first.shape[0]
    pairs = [
        (vol_hbm.at[0:tile], first),
        (vol_hbm.at[rows - tile : rows], last),
        (meas_hbm, meas_ref),
        (start_hbm, start_ref),
        (len_hbm, len_ref),
        (slot_hbm, slot_ref),
    ]
    copies = [pltpu.make_async_copy(*pair, sem.at[i]) for i, pair in enumerate(pairs)]
    for copy in copies:
        copy.start()
    for copy in copies:
        copy.wait()
    orient = lax.axis_index("orient")
    slab = lax.axis_index("slab")
    lanes = lax.broadcasted_iota(jnp.int32, (1, det), 1)

    def line(flag):
        return jnp.full((1, det), jnp.where(flag, 1.0, 0.0), f32)

    for k in range(8):
        begin = start_ref[k]
        inside = (lanes >= begin) & (lanes < begin + len_ref[k])
        table_ref[MASK + k : MASK + k + 1, :] = jnp.where(inside, 1.0, 0.0)
    for s in range(FRAMES):
        image = slot_ref[jnp.bitwise_xor(orient, s)]
        refl = jnp.right_shift(image, 2)
        for k in range(8):
            wanted = k * FRAMES + jnp.bitwise_and(orient + k, FRAMES - 1)
            table_ref[HELD + 8 * s + k : HELD + 8 * s + k + 1, :] = line(image == wanted)
            table_ref[PICK + 8 * s + k : PICK + 8 * s + k + 1, :] = line(refl == k)
    mine = slot_ref[orient]
    source = jnp.bitwise_and(jnp.bitwise_xor(mine - jnp.right_shift(mine, 2), orient), FRAMES - 1)
    for s in range(FRAMES):
        table_ref[FROM + s : FROM + s + 1, :] = line(source == s)
    table_ref[SCALE : SCALE + 1, :] = jnp.full((1, det), relax_ref[0] * step_gain, f32)
    table_ref[BOUND : BOUND + 1, :] = line(slab != slabs - 1) * huber_delta
    table_ref[BOUND + 1 : BOUND + 2, :] = line(slab != 0) * huber_delta
    table_ref[BOUND + 2 : BOUND + 3, :] = line(slab < 0)
    low = jnp.concatenate([last[tile - 2 :, :], meas_ref[rows - 2 :, :].astype(bf16)], axis=1)
    high = jnp.concatenate([first[0:2, :], meas_ref[0:2, :].astype(bf16)], axis=1)
    even = jnp.bitwise_and(slab, 1) == 0

    @pl.when(even)
    def _():
        near_ref[...] = low
        far_ref[...] = high

    @pl.when(jnp.logical_not(even))
    def _():
        near_ref[...] = high
        far_ref[...] = low


def prepare(vol, start, length, slot_image, meas, relax, step_gain, slabs):
    rows, cells = vol.shape
    det = meas.shape[1]
    edge = jax.ShapeDtypeStruct((2, cells + det), bf16)
    return pl.pallas_call(
        lambda *refs: prepare_kernel(step_gain, slabs, *refs),
        in_specs=[HBM] * 5 + [SMEM],
        out_specs=(VMEM,) * 4,
        out_shape=(
            edge, edge, jax.ShapeDtypeStruct(meas.shape, f32), jax.ShapeDtypeStruct((TABLE, det), f32)
        ),
        scratch_shapes=[
            pltpu.VMEM((HALO, cells), bf16),
            pltpu.VMEM((HALO, cells), bf16),
            pltpu.SMEM(start.shape, jnp.int32),
            pltpu.SMEM(length.shape, jnp.int32),
            pltpu.SMEM(slot_image.shape, jnp.int32),
            pltpu.SemaphoreType.DMA((6,)),
        ],
        compiler_params=pltpu.CompilerParams(vmem_limit_bytes=SMALL),
        cost_estimate=pl.CostEstimate(flops=40 << 30, transcendentals=0, bytes_accessed=1 << 20),
        name="prepare",
    )(*(keep(x) for x in (vol, meas, start, length, slot_image)), relax)


def halo_rows(near, far, even):
    below = jnp.where(even, near, far)
    above = jnp.where(even, far, near)
    zeros = jnp.zeros((HALO - 4, near.shape[1]), bf16)
    return jnp.concatenate([below, zeros, above], axis=0)


def extend_kernel(meas_ref, near_ref, far_ref, ext_ref):
    rows, det = meas_ref.shape
    cells = near_ref.shape[1] - det
    even = jnp.bitwise_and(lax.axis_index("slab"), 1) == 0
    ext_ref[0:rows] = meas_ref[...].astype(bf16)
    ext_ref[rows:] = halo_rows(near_ref[:, cells:], far_ref[:, cells:], even)


def extend(meas, near, far):
    rows, det = meas.shape
    return pl.pallas_call(
        extend_kernel,
        in_specs=[VMEM] * 3,
        out_specs=VMEM,
        out_shape=jax.ShapeDtypeStruct((rows + HALO, det), bf16),
        compiler_params=pltpu.CompilerParams(vmem_limit_bytes=SMALL),
        name="extend",
    )(meas, near, far)


def project_kernel(vol_hbm, near_ref, far_ref, rays_ref, table_ref, proj_ref, flat_ref, vol_ref, acc, sem):
    rows, cells = vol_hbm.shape
    refl, det = rays_ref.shape[1:]
    chunk = cells // CHUNKS
    copy = pltpu.make_async_copy(vol_hbm, vol_ref.at[0:rows], sem)
    copy.start()
    even = jnp.bitwise_and(lax.axis_index("slab"), 1) == 0
    vol_ref[rows:, :] = halo_rows(near_ref[:, 0:cells], far_ref[:, 0:cells], even)
    for i in range(CHUNKS):
        at = slice(i * chunk, (i + 1) * chunk)
        flat_ref[at, :] = rays_ref[at].reshape(chunk, refl * det)
        if i == 0:
            copy.wait()
        part = jnp.dot(vol_ref[:, at], flat_ref[at, :], preferred_element_type=f32)
        acc[...] = part if i == 0 else acc[...] + part
    for k in range(refl):
        proj_ref[k] = acc[:, k * det : (k + 1) * det] * table_ref[MASK + k : MASK + k + 1, :]


def project(vol, near, far, rays, table):
    rows, cells = vol.shape
    refl, det = rays.shape[1:]
    ext = rows + HALO
    return pl.pallas_call(
        project_kernel,
        in_specs=[HBM, VMEM, VMEM, VMEM, VMEM],
        out_specs=(VMEM, VMEM, VMEM),
        out_shape=(
            jax.ShapeDtypeStruct((refl, ext, det), f32),
            pltpu.VMEM((cells, refl * det), bf16),
            pltpu.VMEM((ext, cells), bf16),
        ),
        scratch_shapes=[pltpu.VMEM((ext, refl * det), f32), pltpu.SemaphoreType.DMA],
        compiler_params=pltpu.CompilerParams(vmem_limit_bytes=8 << 20),
        name="project",
    )(keep(vol), near, far, rays, table)


def combine_kernel(proj_ref, table_ref, *refs):
    gathered, part_ref = refs[:FRAMES], refs[FRAMES]
    images = [ref[...].astype(f32) for ref in gathered]
    for k in range(proj_ref.shape[0]):
        part = proj_ref[k]
        for s in range(FRAMES):
            row = HELD + 8 * s + k
            part = part - table_ref[row : row + 1, :] * images[s]
        part_ref[k] = part.astype(bf16)


def combine(proj, table, gathered):
    return pl.pallas_call(
        combine_kernel,
        in_specs=[VMEM] * (2 + FRAMES),
        out_specs=VMEM,
        out_shape=jax.ShapeDtypeStruct(proj.shape, bf16),
        compiler_params=pltpu.CompilerParams(vmem_limit_bytes=SMALL),
        name="combine",
    )(proj, table, *gathered)


def total_kernel(pieces_ref, out_ref):
    count = pieces_ref.shape[0]
    total = pieces_ref[0].astype(f32)
    for i in range(1, count):
        total = total + pieces_ref[i].astype(f32)
    own = (-total).astype(bf16)
    for i in range(count):
        out_ref[i] = own


def total(pieces):
    return pl.pallas_call(
        total_kernel,
        in_specs=[VMEM],
        out_specs=VMEM,
        out_shape=jax.ShapeDtypeStruct(pieces.shape, bf16),
        compiler_params=pltpu.CompilerParams(vmem_limit_bytes=SMALL),
        name="total",
    )(pieces)


def pick_kernel(img_ref, table_ref, *outs):
    rows = outs[0].shape[0]
    for s in range(FRAMES):
        image = jnp.zeros(outs[0].shape, f32)
        for k in range(img_ref.shape[0]):
            row = PICK + 8 * s + k
            image = image + table_ref[row : row + 1, :] * img_ref[k, 0:rows, :].astype(f32)
        outs[s][...] = image.astype(bf16)


def pick(img, table, rows):
    shape = jax.ShapeDtypeStruct((rows, img.shape[2]), bf16)
    return pl.pallas_call(
        pick_kernel,
        in_specs=[VMEM, VMEM],
        out_specs=(VMEM,) * FRAMES,
        out_shape=(shape,) * FRAMES,
        compiler_params=pltpu.CompilerParams(vmem_limit_bytes=SMALL),
        name="pick",
    )(img, table)


def choose_kernel(table_ref, *refs):
    image = jnp.zeros(refs[0].shape, f32)
    for s in range(FRAMES):
        image = image + table_ref[FROM + s : FROM + s + 1, :] * refs[s][...].astype(f32)
    refs[FRAMES][...] = image


def choose(table, images):
    return pl.pallas_call(
        choose_kernel,
        in_specs=[VMEM] * (1 + FRAMES),
        out_specs=VMEM,
        out_shape=jax.ShapeDtypeStruct(images[0].shape, f32),
        compiler_params=pltpu.CompilerParams(vmem_limit_bytes=SMALL),
        name="choose",
    )(table, *images)


def update_kernel(img_ref, table_ref, flat_ref, vol_ref, out_hbm, dbuf, fbuf, obuf, osem):
    refl, ext, det = img_ref.shape
    cells = vol_ref.shape[1]
    rows = ext - HALO
    slots = dbuf.shape[0]
    tiles = slots // 2
    chunk = tiles * det
    steps = cells // chunk
    sends = osem.shape[0]

    img = jnp.concatenate(
        [img_ref[k] * table_ref[MASK + k : MASK + k + 1, :].astype(bf16) for k in range(refl)], axis=1
    )
    scale = table_ref[SCALE : SCALE + 1, 0:1]

    place = lax.broadcasted_iota(jnp.int32, (ext, det), 0)
    bound = jnp.where(
        place == rows + 7,
        table_ref[BOUND : BOUND + 1, :],
        jnp.where(place == 7, table_ref[BOUND + 1 : BOUND + 2, :], huber_delta),
    )
    zeros = jnp.zeros((8, det), f32)
    for q in range(slots):
        dbuf[q, 0:8] = zeros
        dbuf[q, 8 + ext :] = zeros
        fbuf[q, 0:8] = zeros

    def psi(t, first):
        limit = bound[first : first + t.shape[0]]
        return jnp.minimum(jnp.maximum(t, -limit), limit)

    def backproject(i):
        at = slice(i * chunk, (i + 1) * chunk)
        gradient = lax.dot_general(
            img, flat_ref[at, :], (((1,), (1,)), ((), ())), preferred_element_type=f32
        )
        density = vol_ref[:, at].astype(f32) + scale * gradient
        for t in range(tiles):
            q = (i * tiles + t) % slots
            lanes = slice(t * det, (t + 1) * det)
            dbuf[q, 8:16] = density[ext - 8 :, lanes]
            dbuf[q, 16 : 8 + ext] = density[0 : ext - 8, lanes]

    def out_copy(j):
        at = slice(j * (cells // sends), (j + 1) * (cells // sends))
        return pltpu.make_async_copy(obuf.at[:, at], out_hbm.at[:, at], osem.at[j])

    def smooth(i):
        for t in range(tiles):
            q = (i * tiles + t) % slots
            here = dbuf[q, 8 : 8 + ext]
            flux = psi(dbuf[q, 9 : 9 + ext] - here, 0)
            fbuf[q, 8 : 8 + ext] = flux
            once = here + sweep_rate * (flux - fbuf[q, 7 : 7 + ext])
            dbuf[q, 8 : 8 + ext] = once
            fbuf[q, 8 : 16 + rows] = psi(dbuf[q, 9 : 17 + rows] - once[0 : 8 + rows], 0)
            net = fbuf[q, 16 : 16 + rows] - fbuf[q, 15 : 15 + rows]
            at = slice(i * chunk + t * det, i * chunk + (t + 1) * det)
            obuf[:, at] = (once[8 : 8 + rows] + sweep_rate * net).astype(bf16)
        if (i + 1) * sends % steps == 0:
            out_copy((i + 1) * sends // steps - 1).start()

    backproject(0)
    for i in range(1, steps):
        backproject(i)
        smooth(i - 1)
    smooth(steps - 1)
    for j in range(sends):
        out_copy(j).wait()


def update(img, table, flat, vol_ext, chunk=256, sends=8):
    ext, cells = vol_ext.shape
    rows = ext - HALO
    det = img.shape[2]
    slot = pltpu.VMEM((2 * chunk // det, ext + 16, det), f32)
    return pl.pallas_call(
        update_kernel,
        in_specs=[VMEM] * 4,
        out_specs=HBM,
        out_shape=jax.ShapeDtypeStruct((rows, cells), bf16),
        scratch_shapes=[slot, slot, pltpu.VMEM((rows, cells), bf16), pltpu.SemaphoreType.DMA((sends,))],
        compiler_params=pltpu.CompilerParams(vmem_limit_bytes=8 << 20),
        name="update",
    )(img, table, flat, vol_ext)


def local(volume, rays, band_start, band_len, slot_image, measured, relax):
    cells, refl, det = rays.shape
    rows = volume.shape[1]
    slabs = lax.axis_size("slab")
    orients = lax.axis_size("orient")
    members = orients // FRAMES
    classes = [[g * FRAMES + q for g in range(members)] for q in range(FRAMES)]
    vol = volume[0]
    meas = measured[0]
    step_gain = math.sqrt(cells * orients / (FRAMES * refl * det))

    near, far, meas, table = prepare(
        vol, band_start[:, 0], band_len[:, 0], slot_image, meas, relax, step_gain, slabs
    )

    near = lax.ppermute(near, "slab", [(i, i ^ 1) for i in range(slabs)])
    far = lax.ppermute(far, "slab", [(i, slabs - 1 - i) for i in range(slabs)])
    meas_ext = extend(meas, near, far)

    swaps = [[(o, o ^ s) for o in range(orients)] for s in range(FRAMES)]
    gathered = [meas_ext] + [lax.ppermute(meas_ext, "orient", swaps[s]) for s in range(1, FRAMES)]

    proj, flat, vol_ext = project(vol, near, far, rays, table)

    part = combine(proj, table, gathered)
    pieces = lax.all_to_all(part, "orient", 0, 0, axis_index_groups=classes, tiled=True)
    images = lax.all_to_all(total(pieces), "orient", 0, 0, axis_index_groups=classes, tiled=True)

    picked = pick(images, table, rows)
    arrived = [picked[0]] + [lax.ppermute(picked[s], "orient", swaps[s]) for s in range(1, FRAMES)]
    updated = update(images, table, flat, vol_ext)
    residual = choose(table, arrived)
    return (updated[None], residual[None])


def solution(mesh):
    placed = (
        P("orient", "slab", None),
        P(),
        P(None, "orient"),
        P(None, "orient"),
        P(),
        P("orient", "slab", None),
        P("orient"),
    )
    return jax.shard_map(
        local,
        mesh=mesh,
        in_specs=placed,
        out_specs=(P("orient", "slab", None), P("orient", "slab", None)),
        check_vma=False,
    )
```

```python
import math

import jax
import jax.numpy as jnp
from jax import lax
from jax.experimental import pallas as pl
from jax.experimental.pallas import tpu as pltpu
from jax.sharding import PartitionSpec as P

FRAMES = 4
SWEEPS = 2
HALO = 16

huber_delta = 0.5
sweep_rate = 0.2

bf16 = jnp.bfloat16
f32 = jnp.float32


CHUNKS = 8
PIECE = 16
SMALL = 4 << 20

MASK = 0
HELD = 8
PICK = 40
FROM = 72
SCALE = 76
BOUND = 77
TABLE = 80

VMEM = pl.BlockSpec(memory_space=pltpu.VMEM)
SMEM = pl.BlockSpec(memory_space=pltpu.SMEM)
HBM = pl.BlockSpec(memory_space=pltpu.HBM)


def keep(x):
    return pltpu.with_memory_space_constraint(x, pltpu.HBM)


def prepare_kernel(step_gain, slabs, vol_hbm, meas_hbm, start_hbm, len_hbm, slot_hbm, relax_ref,
                   near_ref, far_ref, meas_ref, table_ref,
                   first, last, start_ref, len_ref, slot_ref, sem):
    rows, cells = vol_hbm.shape
    det = meas_ref.shape[1]
    tile = first.shape[0]
    pairs = [
        (vol_hbm.at[0:tile], first),
        (vol_hbm.at[rows - tile : rows], last),
        (meas_hbm, meas_ref),
        (start_hbm, start_ref),
        (len_hbm, len_ref),
        (slot_hbm, slot_ref),
    ]
    copies = [pltpu.make_async_copy(*pair, sem.at[i]) for i, pair in enumerate(pairs)]
    for copy in copies:
        copy.start()
    for copy in copies:
        copy.wait()
    orient = lax.axis_index("orient")
    slab = lax.axis_index("slab")
    lanes = lax.broadcasted_iota(jnp.int32, (1, det), 1)

    def line(flag):
        return jnp.full((1, det), jnp.where(flag, 1.0, 0.0), f32)

    for k in range(8):
        begin = start_ref[k]
        inside = (lanes >= begin) & (lanes < begin + len_ref[k])
        table_ref[MASK + k : MASK + k + 1, :] = jnp.where(inside, 1.0, 0.0)
    for s in range(FRAMES):
        image = slot_ref[jnp.bitwise_xor(orient, s)]
        refl = jnp.right_shift(image, 2)
        for k in range(8):
            wanted = k * FRAMES + jnp.bitwise_and(orient + k, FRAMES - 1)
            table_ref[HELD + 8 * s + k : HELD + 8 * s + k + 1, :] = line(image == wanted)
            table_ref[PICK + 8 * s + k : PICK + 8 * s + k + 1, :] = line(refl == k)
    mine = slot_ref[orient]
    source = jnp.bitwise_and(jnp.bitwise_xor(mine - jnp.right_shift(mine, 2), orient), FRAMES - 1)
    for s in range(FRAMES):
        table_ref[FROM + s : FROM + s + 1, :] = line(source == s)
    table_ref[SCALE : SCALE + 1, :] = jnp.full((1, det), relax_ref[0] * step_gain, f32)
    table_ref[BOUND : BOUND + 1, :] = line(slab != slabs - 1) * huber_delta
    table_ref[BOUND + 1 : BOUND + 2, :] = line(slab != 0) * huber_delta
    table_ref[BOUND + 2 : BOUND + 3, :] = line(slab < 0)
    low = jnp.concatenate([last[tile - 2 :, :], meas_ref[rows - 2 :, :].astype(bf16)], axis=1)
    high = jnp.concatenate([first[0:2, :], meas_ref[0:2, :].astype(bf16)], axis=1)
    even = jnp.bitwise_and(slab, 1) == 0

    @pl.when(even)
    def _():
        near_ref[...] = low
        far_ref[...] = high

    @pl.when(jnp.logical_not(even))
    def _():
        near_ref[...] = high
        far_ref[...] = low


def prepare(vol, start, length, slot_image, meas, relax, step_gain, slabs):
    rows, cells = vol.shape
    det = meas.shape[1]
    edge = jax.ShapeDtypeStruct((2, cells + det), bf16)
    return pl.pallas_call(
        lambda *refs: prepare_kernel(step_gain, slabs, *refs),
        in_specs=[HBM] * 5 + [SMEM],
        out_specs=(VMEM,) * 4,
        out_shape=(
            edge, edge, jax.ShapeDtypeStruct(meas.shape, f32), jax.ShapeDtypeStruct((TABLE, det), f32)
        ),
        scratch_shapes=[
            pltpu.VMEM((HALO, cells), bf16),
            pltpu.VMEM((HALO, cells), bf16),
            pltpu.SMEM(start.shape, jnp.int32),
            pltpu.SMEM(length.shape, jnp.int32),
            pltpu.SMEM(slot_image.shape, jnp.int32),
            pltpu.SemaphoreType.DMA((6,)),
        ],
        compiler_params=pltpu.CompilerParams(vmem_limit_bytes=SMALL),
        cost_estimate=pl.CostEstimate(flops=40 << 30, transcendentals=0, bytes_accessed=1 << 20),
        name="prepare",
    )(*(keep(x) for x in (vol, meas, start, length, slot_image)), relax)


def halo_rows(near, far, even):
    below = jnp.where(even, near, far)
    above = jnp.where(even, far, near)
    zeros = jnp.zeros((HALO - 4, near.shape[1]), bf16)
    return jnp.concatenate([below, zeros, above], axis=0)


def extend_kernel(meas_ref, near_ref, far_ref, ext_ref):
    rows, det = meas_ref.shape
    cells = near_ref.shape[1] - det
    even = jnp.bitwise_and(lax.axis_index("slab"), 1) == 0
    ext_ref[0:rows] = meas_ref[...].astype(bf16)
    ext_ref[rows:] = halo_rows(near_ref[:, cells:], far_ref[:, cells:], even)


def extend(meas, near, far):
    rows, det = meas.shape
    return pl.pallas_call(
        extend_kernel,
        in_specs=[VMEM] * 3,
        out_specs=VMEM,
        out_shape=jax.ShapeDtypeStruct((rows + HALO, det), bf16),
        compiler_params=pltpu.CompilerParams(vmem_limit_bytes=SMALL),
        name="extend",
    )(meas, near, far)


def project_kernel(vol_hbm, near_ref, far_ref, rays_ref, table_ref, proj_ref, flat_ref, vol_ref, acc, sem):
    rows, cells = vol_hbm.shape
    refl, det = rays_ref.shape[1:]
    chunk = cells // CHUNKS
    copy = pltpu.make_async_copy(vol_hbm, vol_ref.at[0:rows], sem)
    copy.start()
    even = jnp.bitwise_and(lax.axis_index("slab"), 1) == 0
    vol_ref[rows:, :] = halo_rows(near_ref[:, 0:cells], far_ref[:, 0:cells], even)
    low = lax.broadcasted_iota(jnp.int32, (1, det), 1) < det // 2
    low_block = jnp.broadcast_to(low, (PIECE, det))
    stay = []
    for k in range(MASK, MASK + refl, 2):
        line = jnp.where(low, table_ref[k : k + 1, :], table_ref[k + 1 : k + 2, :])
        stay.append(jnp.broadcast_to(line.astype(bf16), (PIECE, det)) > 0.5)
    for i in range(CHUNKS):
        at = slice(i * chunk, (i + 1) * chunk)
        for j in range(i * chunk, (i + 1) * chunk, PIECE):
            flat = rays_ref[j : j + PIECE].reshape(PIECE, refl * det)
            for p, keeps in enumerate(stay):
                first = flat[:, 2 * p * det : (2 * p + 1) * det]
                second = flat[:, (2 * p + 1) * det : (2 * p + 2) * det]
                straight = jnp.where(low_block, first, second)
                crossed = jnp.where(low_block, second, first)
                flat_ref[j : j + PIECE, p * det : (p + 1) * det] = jnp.where(
                    keeps, straight, pltpu.roll(crossed, det // 2, 1)
                )
        if i == 0:
            copy.wait()
        part = jnp.dot(vol_ref[:, at], flat_ref[at, :], preferred_element_type=f32)
        acc[...] = part if i == 0 else acc[...] + part
    for k in range(0, refl, 2):
        both = acc[:, k // 2 * det : (k // 2 + 1) * det]
        swapped = pltpu.roll(both, det // 2, 1)
        proj_ref[k] = jnp.where(low, both, swapped) * table_ref[MASK + k : MASK + k + 1, :]
        proj_ref[k + 1] = jnp.where(low, swapped, both) * table_ref[MASK + k + 1 : MASK + k + 2, :]


def project(vol, near, far, rays, table):
    rows, cells = vol.shape
    refl, det = rays.shape[1:]
    ext = rows + HALO
    return pl.pallas_call(
        project_kernel,
        in_specs=[HBM, VMEM, VMEM, VMEM, VMEM],
        out_specs=(VMEM, VMEM, VMEM),
        out_shape=(
            jax.ShapeDtypeStruct((refl, ext, det), f32),
            pltpu.VMEM((cells, refl * det // 2), bf16),
            pltpu.VMEM((ext, cells), bf16),
        ),
        scratch_shapes=[pltpu.VMEM((ext, refl * det // 2), f32), pltpu.SemaphoreType.DMA],
        compiler_params=pltpu.CompilerParams(vmem_limit_bytes=8 << 20),
        name="project",
    )(keep(vol), near, far, rays, table)


def combine_kernel(proj_ref, table_ref, *refs):
    gathered, part_ref = refs[:FRAMES], refs[FRAMES]
    images = [ref[...].astype(f32) for ref in gathered]
    for k in range(proj_ref.shape[0]):
        part = proj_ref[k]
        for s in range(FRAMES):
            row = HELD + 8 * s + k
            part = part - table_ref[row : row + 1, :] * images[s]
        part_ref[k] = part.astype(bf16)


def combine(proj, table, gathered):
    return pl.pallas_call(
        combine_kernel,
        in_specs=[VMEM] * (2 + FRAMES),
        out_specs=VMEM,
        out_shape=jax.ShapeDtypeStruct(proj.shape, bf16),
        compiler_params=pltpu.CompilerParams(vmem_limit_bytes=SMALL),
        name="combine",
    )(proj, table, *gathered)


def total_kernel(pieces_ref, out_ref):
    count = pieces_ref.shape[0]
    total = pieces_ref[0].astype(f32)
    for i in range(1, count):
        total = total + pieces_ref[i].astype(f32)
    own = (-total).astype(bf16)
    for i in range(count):
        out_ref[i] = own


def total(pieces):
    return pl.pallas_call(
        total_kernel,
        in_specs=[VMEM],
        out_specs=VMEM,
        out_shape=jax.ShapeDtypeStruct(pieces.shape, bf16),
        compiler_params=pltpu.CompilerParams(vmem_limit_bytes=SMALL),
        name="total",
    )(pieces)


def pick_kernel(img_ref, table_ref, *outs):
    rows = outs[0].shape[0]
    for s in range(FRAMES):
        image = jnp.zeros(outs[0].shape, f32)
        for k in range(img_ref.shape[0]):
            row = PICK + 8 * s + k
            image = image + table_ref[row : row + 1, :] * img_ref[k, 0:rows, :].astype(f32)
        outs[s][...] = image.astype(bf16)


def pick(img, table, rows):
    shape = jax.ShapeDtypeStruct((rows, img.shape[2]), bf16)
    return pl.pallas_call(
        pick_kernel,
        in_specs=[VMEM, VMEM],
        out_specs=(VMEM,) * FRAMES,
        out_shape=(shape,) * FRAMES,
        compiler_params=pltpu.CompilerParams(vmem_limit_bytes=SMALL),
        name="pick",
    )(img, table)


def choose_kernel(table_ref, *refs):
    image = jnp.zeros(refs[0].shape, f32)
    for s in range(FRAMES):
        image = image + table_ref[FROM + s : FROM + s + 1, :] * refs[s][...].astype(f32)
    refs[FRAMES][...] = image


def choose(table, images):
    return pl.pallas_call(
        choose_kernel,
        in_specs=[VMEM] * (1 + FRAMES),
        out_specs=VMEM,
        out_shape=jax.ShapeDtypeStruct(images[0].shape, f32),
        compiler_params=pltpu.CompilerParams(vmem_limit_bytes=SMALL),
        name="choose",
    )(table, *images)


def update_kernel(img_ref, table_ref, flat_ref, vol_ref, out_hbm, dbuf, fbuf, obuf, osem):
    refl, ext, det = img_ref.shape
    cells = vol_ref.shape[1]
    rows = ext - HALO
    slots = dbuf.shape[0]
    tiles = slots // 2
    chunk = tiles * det
    steps = cells // chunk
    sends = osem.shape[0]

    low = lax.broadcasted_iota(jnp.int32, (1, det), 1) < det // 2
    parts = []
    for k in range(0, refl, 2):
        first = img_ref[k].astype(f32) * table_ref[MASK + k : MASK + k + 1, :]
        second = img_ref[k + 1].astype(f32) * table_ref[MASK + k + 1 : MASK + k + 2, :]
        straight = jnp.where(low, first, second)
        crossed = jnp.where(low, second, first)
        parts.append((straight + pltpu.roll(crossed, det // 2, 1)).astype(bf16))
    img = jnp.concatenate(parts, axis=1)
    scale = table_ref[SCALE : SCALE + 1, 0:1]

    place = lax.broadcasted_iota(jnp.int32, (ext, det), 0)
    bound = jnp.where(
        place == rows + 7,
        table_ref[BOUND : BOUND + 1, :],
        jnp.where(place == 7, table_ref[BOUND + 1 : BOUND + 2, :], huber_delta),
    )
    zeros = jnp.zeros((8, det), f32)
    for q in range(slots):
        dbuf[q, 0:8] = zeros
        dbuf[q, 8 + ext :] = zeros
        fbuf[q, 0:8] = zeros

    def psi(t, first):
        limit = bound[first : first + t.shape[0]]
        return jnp.minimum(jnp.maximum(t, -limit), limit)

    def backproject(i):
        at = slice(i * chunk, (i + 1) * chunk)
        gradient = lax.dot_general(
            img, flat_ref[at, :], (((1,), (1,)), ((), ())), preferred_element_type=f32
        )
        density = vol_ref[:, at].astype(f32) + scale * gradient
        for t in range(tiles):
            q = (i * tiles + t) % slots
            lanes = slice(t * det, (t + 1) * det)
            dbuf[q, 8:16] = density[ext - 8 :, lanes]
            dbuf[q, 16 : 8 + ext] = density[0 : ext - 8, lanes]

    def out_copy(j):
        at = slice(j * (cells // sends), (j + 1) * (cells // sends))
        return pltpu.make_async_copy(obuf.at[:, at], out_hbm.at[:, at], osem.at[j])

    def smooth(i):
        for t in range(tiles):
            q = (i * tiles + t) % slots
            here = dbuf[q, 8 : 8 + ext]
            flux = psi(dbuf[q, 9 : 9 + ext] - here, 0)
            fbuf[q, 8 : 8 + ext] = flux
            once = here + sweep_rate * (flux - fbuf[q, 7 : 7 + ext])
            dbuf[q, 8 : 8 + ext] = once
            fbuf[q, 8 : 16 + rows] = psi(dbuf[q, 9 : 17 + rows] - once[0 : 8 + rows], 0)
            net = fbuf[q, 16 : 16 + rows] - fbuf[q, 15 : 15 + rows]
            at = slice(i * chunk + t * det, i * chunk + (t + 1) * det)
            obuf[:, at] = (once[8 : 8 + rows] + sweep_rate * net).astype(bf16)
        if (i + 1) * sends % steps == 0:
            out_copy((i + 1) * sends // steps - 1).start()

    backproject(0)
    for i in range(1, steps):
        backproject(i)
        smooth(i - 1)
    smooth(steps - 1)
    for j in range(sends):
        out_copy(j).wait()


def update(img, table, flat, vol_ext, chunk=256, sends=8):
    ext, cells = vol_ext.shape
    rows = ext - HALO
    det = img.shape[2]
    slot = pltpu.VMEM((2 * chunk // det, ext + 16, det), f32)
    return pl.pallas_call(
        update_kernel,
        in_specs=[VMEM] * 4,
        out_specs=HBM,
        out_shape=jax.ShapeDtypeStruct((rows, cells), bf16),
        scratch_shapes=[slot, slot, pltpu.VMEM((rows, cells), bf16), pltpu.SemaphoreType.DMA((sends,))],
        compiler_params=pltpu.CompilerParams(vmem_limit_bytes=8 << 20),
        name="update",
    )(img, table, flat, vol_ext)


def local(volume, rays, band_start, band_len, slot_image, measured, relax):
    cells, refl, det = rays.shape
    rows = volume.shape[1]
    slabs = lax.axis_size("slab")
    orients = lax.axis_size("orient")
    members = orients // FRAMES
    classes = [[g * FRAMES + q for g in range(members)] for q in range(FRAMES)]
    vol = volume[0]
    meas = measured[0]
    step_gain = math.sqrt(cells * orients / (FRAMES * refl * det))

    near, far, meas, table = prepare(
        vol, band_start[:, 0], band_len[:, 0], slot_image, meas, relax, step_gain, slabs
    )

    near = lax.ppermute(near, "slab", [(i, i ^ 1) for i in range(slabs)])
    far = lax.ppermute(far, "slab", [(i, slabs - 1 - i) for i in range(slabs)])
    meas_ext = extend(meas, near, far)

    swaps = [[(o, o ^ s) for o in range(orients)] for s in range(FRAMES)]
    gathered = [meas_ext] + [lax.ppermute(meas_ext, "orient", swaps[s]) for s in range(1, FRAMES)]

    proj, flat, vol_ext = project(vol, near, far, rays, table)

    part = combine(proj, table, gathered)
    pieces = lax.all_to_all(part, "orient", 0, 0, axis_index_groups=classes, tiled=True)
    images = lax.all_to_all(total(pieces), "orient", 0, 0, axis_index_groups=classes, tiled=True)

    picked = pick(images, table, rows)
    arrived = [picked[0]] + [lax.ppermute(picked[s], "orient", swaps[s]) for s in range(1, FRAMES)]
    updated = update(images, table, flat, vol_ext)
    residual = choose(table, arrived)
    return (updated[None], residual[None])


def solution(mesh):
    placed = (
        P("orient", "slab", None),
        P(),
        P(None, "orient"),
        P(None, "orient"),
        P(),
        P("orient", "slab", None),
        P("orient"),
    )
    return jax.shard_map(
        local,
        mesh=mesh,
        in_specs=placed,
        out_specs=(P("orient", "slab", None), P("orient", "slab", None)),
        check_vma=False,
    )
```

```python
import math

import jax
import jax.numpy as jnp
from jax import lax
from jax.experimental import pallas as pl
from jax.experimental.pallas import tpu as pltpu
from jax.sharding import PartitionSpec as P


FRAMES = 4
HALO = 16

huber_delta = 0.5
sweep_rate = 0.2

bf16 = jnp.bfloat16
f32 = jnp.float32


CHUNK = 1024
EARLY = 4096
PIECE = 16
SMALL = 4 << 20

MASK = 0
HELD = 8
PICK = 40
FROM = 72
SCALE = 76
BOUND = 77
TABLE = 80

VMEM = pl.BlockSpec(memory_space=pltpu.VMEM)
SMEM = pl.BlockSpec(memory_space=pltpu.SMEM)
HBM = pl.BlockSpec(memory_space=pltpu.HBM)


def keep(x):
    return pltpu.with_memory_space_constraint(x, pltpu.HBM)


def prepare_kernel(step_gain, slabs, vol_hbm, start_hbm, len_hbm, slot_hbm, meas_hbm, relax_ref,
                   low_ref, high_ref, meas_ref, table_ref,
                   first, last, meas, start_ref, len_ref, slot_ref, sem):
    rows = vol_hbm.shape[0]
    det = table_ref.shape[1]
    tile = first.shape[0]
    pairs = [
        (start_hbm, start_ref),
        (len_hbm, len_ref),
        (slot_hbm, slot_ref),
        (vol_hbm.at[0:tile], first),
        (vol_hbm.at[rows - tile : rows], last),
        (meas_hbm, meas),
    ]
    copies = [pltpu.make_async_copy(*pair, sem.at[i]) for i, pair in enumerate(pairs)]
    for copy in copies:
        copy.start()
    for copy in copies[:3]:
        copy.wait()
    orient = lax.axis_index("orient")
    slab = lax.axis_index("slab")
    lanes = lax.broadcasted_iota(jnp.int32, (1, det), 1)

    def line(flag):
        return jnp.full((1, det), jnp.where(flag, 1.0, 0.0), f32)

    for k in range(8):
        begin = start_ref[k]
        inside = (lanes >= begin) & (lanes < begin + len_ref[k])
        table_ref[MASK + k : MASK + k + 1, :] = jnp.where(inside, 1.0, 0.0)
    for s in range(FRAMES):
        image = slot_ref[jnp.bitwise_xor(orient, s)]
        refl = jnp.right_shift(image, 2)
        for k in range(8):
            wanted = k * FRAMES + jnp.bitwise_and(orient + k, FRAMES - 1)
            table_ref[HELD + 8 * s + k : HELD + 8 * s + k + 1, :] = line(image == wanted)
            table_ref[PICK + 8 * s + k : PICK + 8 * s + k + 1, :] = line(refl == k)
    mine = slot_ref[orient]
    source = jnp.bitwise_and(jnp.bitwise_xor(mine - jnp.right_shift(mine, 2), orient), FRAMES - 1)
    for s in range(FRAMES):
        table_ref[FROM + s : FROM + s + 1, :] = line(source == s)
    table_ref[SCALE : SCALE + 1, :] = jnp.full((1, det), relax_ref[0] * step_gain, f32)
    table_ref[BOUND : BOUND + 1, :] = line(slab != slabs - 1) * huber_delta
    table_ref[BOUND + 1 : BOUND + 2, :] = line(slab != 0) * huber_delta
    table_ref[BOUND + 2 : BOUND + 3, :] = line(slab < 0)
    for copy in copies[3:]:
        copy.wait()
    high_ref[...] = first[0:2, :]
    low_ref[...] = last[tile - 2 :, :]
    meas_ref[...] = meas[...].astype(bf16)


def prepare(vol, start, length, slot_image, meas, relax, step_gain, slabs):
    cells = vol.shape[1]
    det = meas.shape[1]
    edge = jax.ShapeDtypeStruct((2, cells), bf16)
    return pl.pallas_call(
        lambda *refs: prepare_kernel(step_gain, slabs, *refs),
        in_specs=[HBM] * 5 + [SMEM],
        out_specs=(VMEM,) * 4,
        out_shape=(
            edge, edge, jax.ShapeDtypeStruct(meas.shape, bf16), jax.ShapeDtypeStruct((TABLE, det), f32)
        ),
        scratch_shapes=[
            pltpu.VMEM((HALO, cells), bf16),
            pltpu.VMEM((HALO, cells), bf16),
            pltpu.VMEM(meas.shape, f32),
            pltpu.SMEM(start.shape, jnp.int32),
            pltpu.SMEM(length.shape, jnp.int32),
            pltpu.SMEM(slot_image.shape, jnp.int32),
            pltpu.SemaphoreType.DMA((6,)),
        ],
        compiler_params=pltpu.CompilerParams(vmem_limit_bytes=SMALL),
        cost_estimate=pl.CostEstimate(flops=40 << 30, transcendentals=0, bytes_accessed=1 << 20),
        name="prepare",
    )(*(keep(x) for x in (vol, start, length, slot_image, meas)), relax)


def pack_kernel(low_ref, high_ref, *refs):
    gathered, near_ref, far_ref = refs[:FRAMES], refs[FRAMES], refs[FRAMES + 1]
    rows = gathered[0].shape[0]
    low = jnp.concatenate([low_ref[...]] + [g[rows - 2 :, :].astype(bf16) for g in gathered], axis=1)
    high = jnp.concatenate([high_ref[...]] + [g[0:2, :].astype(bf16) for g in gathered], axis=1)
    even = jnp.bitwise_and(lax.axis_index("slab"), 1) == 0

    @pl.when(even)
    def _():
        near_ref[...] = low
        far_ref[...] = high

    @pl.when(jnp.logical_not(even))
    def _():
        near_ref[...] = high
        far_ref[...] = low


def pack(low, high, gathered):
    shape = jax.ShapeDtypeStruct((2, low.shape[1] + FRAMES * gathered[0].shape[1]), bf16)
    return pl.pallas_call(
        pack_kernel,
        in_specs=[VMEM] * (2 + FRAMES),
        out_specs=(VMEM, VMEM),
        out_shape=(shape, shape),
        compiler_params=pltpu.CompilerParams(vmem_limit_bytes=SMALL),
        name="pack",
    )(low, high, *gathered)


def halo_rows(near, far, even):
    below = jnp.where(even, near, far)
    above = jnp.where(even, far, near)
    zeros = jnp.zeros((HALO - 4, near.shape[1]), bf16)
    return jnp.concatenate([below, zeros, above], axis=0)


def relay(rays_ref, table_ref, flat_ref, begin, count, skip):
    refl, det = rays_ref.shape[1:]
    low = lax.broadcasted_iota(jnp.int32, (1, det), 1) < det // 2
    low_block = jnp.broadcast_to(low, (PIECE, det))
    stay = []
    for k in range(MASK, MASK + refl, 2):
        line = jnp.where(low, table_ref[k : k + 1, :], table_ref[k + 1 : k + 2, :])
        stay.append(jnp.broadcast_to(line.astype(bf16), (PIECE, det)) > 0.5)
    for j in range(begin, begin + count, PIECE):
        flat = rays_ref[skip + j : skip + j + PIECE].reshape(PIECE, refl * det)
        for p, keeps in enumerate(stay):
            first = flat[:, 2 * p * det : (2 * p + 1) * det]
            second = flat[:, (2 * p + 1) * det : (2 * p + 2) * det]
            straight = jnp.where(low_block, first, second)
            crossed = jnp.where(low_block, second, first)
            flat_ref[j : j + PIECE, p * det : (p + 1) * det] = jnp.where(
                keeps, straight, pltpu.roll(crossed, det // 2, 1)
            )


def relay_kernel(rays_ref, table_ref, flat_ref):
    relay(rays_ref, table_ref, flat_ref, 0, flat_ref.shape[0], 0)


def relay_ahead(rays, table):
    _, refl, det = rays.shape
    return pl.pallas_call(
        relay_kernel,
        in_specs=[VMEM, VMEM],
        out_specs=VMEM,
        out_shape=pltpu.VMEM((EARLY, refl * det // 2), bf16),
        compiler_params=pltpu.CompilerParams(vmem_limit_bytes=SMALL),
        name="relay",
    )(rays, table)


def project_kernel(vol_hbm, near_ref, far_ref, ahead_ref, rays_ref, table_ref, proj_ref, flat_ref, vol_ref, acc, sem):
    rows, cells = vol_hbm.shape
    refl, det = rays_ref.shape[1:]
    early = ahead_ref.shape[0]
    copy = pltpu.make_async_copy(vol_hbm, vol_ref.at[0:rows], sem)
    copy.start()
    even = jnp.bitwise_and(lax.axis_index("slab"), 1) == 0
    vol_ref[rows:, :] = halo_rows(near_ref[:, 0:cells], far_ref[:, 0:cells], even)
    for begin in range(0, cells - early, CHUNK):
        relay(rays_ref, table_ref, flat_ref, begin, CHUNK, early)
        if begin == 0:
            copy.wait()
            acc[...] = jnp.dot(vol_ref[:, 0:early], ahead_ref[...], preferred_element_type=f32)
        acc[...] += jnp.dot(
            vol_ref[:, early + begin : early + begin + CHUNK],
            flat_ref[begin : begin + CHUNK, :],
            preferred_element_type=f32,
        )
    low = lax.broadcasted_iota(jnp.int32, (1, det), 1) < det // 2
    for k in range(0, refl, 2):
        both = acc[:, k // 2 * det : (k // 2 + 1) * det]
        swapped = pltpu.roll(both, det // 2, 1)
        proj_ref[k] = jnp.where(low, both, swapped) * table_ref[MASK + k : MASK + k + 1, :]
        proj_ref[k + 1] = jnp.where(low, swapped, both) * table_ref[MASK + k + 1 : MASK + k + 2, :]


def project(vol, near, far, ahead, rays, table):
    rows, cells = vol.shape
    refl, det = rays.shape[1:]
    ext = rows + HALO
    return pl.pallas_call(
        project_kernel,
        in_specs=[HBM] + [VMEM] * 5,
        out_specs=(VMEM, VMEM, VMEM),
        out_shape=(
            jax.ShapeDtypeStruct((refl, ext, det), f32),
            pltpu.VMEM((cells - EARLY, refl * det // 2), bf16),
            pltpu.VMEM((ext, cells), bf16),
        ),
        scratch_shapes=[pltpu.VMEM((ext, refl * det // 2), f32), pltpu.SemaphoreType.DMA],
        compiler_params=pltpu.CompilerParams(vmem_limit_bytes=8 << 20),
        name="project",
    )(keep(vol), near, far, ahead, rays, table)


def combine_kernel(proj_ref, table_ref, near_ref, far_ref, *refs):
    gathered, part_ref = refs[:FRAMES], refs[FRAMES]
    _, det = gathered[0].shape
    cells = near_ref.shape[1] - FRAMES * det
    even = jnp.bitwise_and(lax.axis_index("slab"), 1) == 0
    halo = halo_rows(near_ref[:, cells:], far_ref[:, cells:], even).astype(f32)
    images = [
        jnp.concatenate([ref[...].astype(f32), halo[:, s * det : (s + 1) * det]], axis=0)
        for s, ref in enumerate(gathered)
    ]
    for k in range(proj_ref.shape[0]):
        part = proj_ref[k]
        for s in range(FRAMES):
            row = HELD + 8 * s + k
            part = part - table_ref[row : row + 1, :] * images[s]
        part_ref[k] = part.astype(bf16)


def combine(proj, table, near, far, gathered):
    return pl.pallas_call(
        combine_kernel,
        in_specs=[VMEM] * (4 + FRAMES),
        out_specs=VMEM,
        out_shape=jax.ShapeDtypeStruct(proj.shape, bf16),
        compiler_params=pltpu.CompilerParams(vmem_limit_bytes=SMALL),
        name="combine",
    )(proj, table, near, far, *gathered)


def total_kernel(pieces_ref, out_ref):
    count = pieces_ref.shape[0]
    total = pieces_ref[0].astype(f32)
    for i in range(1, count):
        total = total + pieces_ref[i].astype(f32)
    own = (-total).astype(bf16)
    for i in range(count):
        out_ref[i] = own


def total(pieces):
    return pl.pallas_call(
        total_kernel,
        in_specs=[VMEM],
        out_specs=VMEM,
        out_shape=jax.ShapeDtypeStruct(pieces.shape, bf16),
        compiler_params=pltpu.CompilerParams(vmem_limit_bytes=SMALL),
        name="total",
    )(pieces)


def pick_kernel(img_ref, table_ref, *outs):
    rows = outs[0].shape[0]
    for s in range(FRAMES):
        image = jnp.zeros(outs[0].shape, f32)
        for k in range(img_ref.shape[0]):
            row = PICK + 8 * s + k
            image = image + table_ref[row : row + 1, :] * img_ref[k, 0:rows, :].astype(f32)
        outs[s][...] = image.astype(bf16)


def pick(img, table, rows):
    shape = jax.ShapeDtypeStruct((rows, img.shape[2]), bf16)
    return pl.pallas_call(
        pick_kernel,
        in_specs=[VMEM, VMEM],
        out_specs=(VMEM,) * FRAMES,
        out_shape=(shape,) * FRAMES,
        compiler_params=pltpu.CompilerParams(vmem_limit_bytes=SMALL),
        name="pick",
    )(img, table)


def choose_kernel(table_ref, *refs):
    image = jnp.zeros(refs[0].shape, f32)
    for s in range(FRAMES):
        image = image + table_ref[FROM + s : FROM + s + 1, :] * refs[s][...].astype(f32)
    refs[FRAMES][...] = image


def choose(table, images):
    return pl.pallas_call(
        choose_kernel,
        in_specs=[VMEM] * (1 + FRAMES),
        out_specs=VMEM,
        out_shape=jax.ShapeDtypeStruct(images[0].shape, f32),
        compiler_params=pltpu.CompilerParams(vmem_limit_bytes=SMALL),
        name="choose",
    )(table, *images)


def update_kernel(img_ref, table_ref, ahead_ref, flat_ref, vol_ref, out_hbm, dbuf, fbuf, obuf, osem):
    refl, ext, det = img_ref.shape
    cells = vol_ref.shape[1]
    rows = ext - HALO
    slots = dbuf.shape[0]
    tiles = slots // 2
    chunk = tiles * det
    steps = cells // chunk
    sends = osem.shape[0]

    low = lax.broadcasted_iota(jnp.int32, (1, det), 1) < det // 2
    parts = []
    for k in range(0, refl, 2):
        first = img_ref[k].astype(f32) * table_ref[MASK + k : MASK + k + 1, :]
        second = img_ref[k + 1].astype(f32) * table_ref[MASK + k + 1 : MASK + k + 2, :]
        straight = jnp.where(low, first, second)
        crossed = jnp.where(low, second, first)
        parts.append((straight + pltpu.roll(crossed, det // 2, 1)).astype(bf16))
    img = jnp.concatenate(parts, axis=1)
    scale = table_ref[SCALE : SCALE + 1, 0:1]

    place = lax.broadcasted_iota(jnp.int32, (ext, det), 0)
    bound = jnp.where(
        place == rows + 7,
        table_ref[BOUND : BOUND + 1, :],
        jnp.where(place == 7, table_ref[BOUND + 1 : BOUND + 2, :], huber_delta),
    )
    zeros = jnp.zeros((8, det), f32)
    for q in range(slots):
        dbuf[q, 0:8] = zeros
        dbuf[q, 8 + ext :] = zeros
        fbuf[q, 0:8] = zeros

    def psi(t, first):
        limit = bound[first : first + t.shape[0]]
        return jnp.minimum(jnp.maximum(t, -limit), limit)

    def backproject(i):
        at = slice(i * chunk, (i + 1) * chunk)
        early = ahead_ref.shape[0]
        if i * chunk < early:
            flat = ahead_ref[at, :]
        else:
            flat = flat_ref[i * chunk - early : (i + 1) * chunk - early, :]
        gradient = lax.dot_general(img, flat, (((1,), (1,)), ((), ())), preferred_element_type=f32)
        density = vol_ref[:, at].astype(f32) + scale * gradient
        for t in range(tiles):
            q = (i * tiles + t) % slots
            lanes = slice(t * det, (t + 1) * det)
            dbuf[q, 8:16] = density[ext - 8 :, lanes]
            dbuf[q, 16 : 8 + ext] = density[0 : ext - 8, lanes]

    def out_copy(j):
        at = slice(j * (cells // sends), (j + 1) * (cells // sends))
        return pltpu.make_async_copy(obuf.at[:, at], out_hbm.at[:, at], osem.at[j])

    def smooth(i):
        for t in range(tiles):
            q = (i * tiles + t) % slots
            here = dbuf[q, 8 : 8 + ext]
            flux = psi(dbuf[q, 9 : 9 + ext] - here, 0)
            fbuf[q, 8 : 8 + ext] = flux
            once = here + sweep_rate * (flux - fbuf[q, 7 : 7 + ext])
            dbuf[q, 8 : 8 + ext] = once
            fbuf[q, 8 : 16 + rows] = psi(dbuf[q, 9 : 17 + rows] - once[0 : 8 + rows], 0)
            net = fbuf[q, 16 : 16 + rows] - fbuf[q, 15 : 15 + rows]
            at = slice(i * chunk + t * det, i * chunk + (t + 1) * det)
            obuf[:, at] = (once[8 : 8 + rows] + sweep_rate * net).astype(bf16)
        if (i + 1) * sends % steps == 0:
            out_copy((i + 1) * sends // steps - 1).start()

    backproject(0)
    for i in range(1, steps):
        backproject(i)
        smooth(i - 1)
    smooth(steps - 1)
    for j in range(sends):
        out_copy(j).wait()


def update(img, table, ahead, flat, vol_ext, chunk=256, sends=16):
    ext, cells = vol_ext.shape
    rows = ext - HALO
    det = img.shape[2]
    slot = pltpu.VMEM((2 * chunk // det, ext + 16, det), f32)
    return pl.pallas_call(
        update_kernel,
        in_specs=[VMEM] * 5,
        out_specs=HBM,
        out_shape=jax.ShapeDtypeStruct((rows, cells), bf16),
        scratch_shapes=[slot, slot, pltpu.VMEM((rows, cells), bf16), pltpu.SemaphoreType.DMA((sends,))],
        compiler_params=pltpu.CompilerParams(vmem_limit_bytes=8 << 20),
        name="update",
    )(img, table, ahead, flat, vol_ext)


def local(volume, rays, band_start, band_len, slot_image, measured, relax):
    cells, refl, det = rays.shape
    rows = volume.shape[1]
    slabs = lax.axis_size("slab")
    orients = lax.axis_size("orient")
    members = orients // FRAMES
    classes = [[g * FRAMES + q for g in range(members)] for q in range(FRAMES)]
    vol = volume[0]
    meas = measured[0]
    step_gain = math.sqrt(cells * orients / (FRAMES * refl * det))

    swaps = [[(o, o ^ s) for o in range(orients)] for s in range(FRAMES)]
    low, high, meas, table = prepare(
        vol, band_start[:, 0], band_len[:, 0], slot_image, meas, relax, step_gain, slabs
    )
    gathered = [meas] + [lax.ppermute(meas, "orient", swaps[s]) for s in range(1, FRAMES)]
    near, far = pack(low, high, gathered)

    near = lax.ppermute(near, "slab", [(i, i ^ 1) for i in range(slabs)])
    far = lax.ppermute(far, "slab", [(i, slabs - 1 - i) for i in range(slabs)])
    ahead = relay_ahead(rays, table)
    proj, flat, vol_ext = project(vol, near, far, ahead, rays, table)

    part = combine(proj, table, near, far, gathered)
    pieces = lax.all_to_all(part, "orient", 0, 0, axis_index_groups=classes, tiled=True)
    images = lax.all_to_all(total(pieces), "orient", 0, 0, axis_index_groups=classes, tiled=True)

    picked = pick(images, table, rows)
    arrived = [picked[0]] + [lax.ppermute(picked[s], "orient", swaps[s]) for s in range(1, FRAMES)]
    updated = update(images, table, ahead, flat, vol_ext)
    residual = choose(table, arrived)
    return (updated[None], residual[None])


def solution(mesh):
    placed = (
        P("orient", "slab", None),
        P(),
        P(None, "orient"),
        P(None, "orient"),
        P(),
        P("orient", "slab", None),
        P("orient"),
    )
    return jax.shard_map(
        local,
        mesh=mesh,
        in_specs=placed,
        out_specs=(P("orient", "slab", None), P("orient", "slab", None)),
        check_vma=False,
    )
```

```python
import math

import jax
import jax.numpy as jnp
from jax import lax
from jax.experimental import pallas as pl
from jax.experimental.pallas import tpu as pltpu
from jax.sharding import PartitionSpec as P


FRAMES = 4
HALO = 16

huber_delta = 0.5
sweep_rate = 0.2

bf16 = jnp.bfloat16
f32 = jnp.float32


CHUNK = 1024
EARLY = 6144
PIECE = 16
SMALL = 4 << 20

MASK = 0
HELD = 8
PICK = 40
FROM = 72
SCALE = 76
BOUND = 77
TABLE = 80

VMEM = pl.BlockSpec(memory_space=pltpu.VMEM)
SMEM = pl.BlockSpec(memory_space=pltpu.SMEM)
HBM = pl.BlockSpec(memory_space=pltpu.HBM)


def keep(x):
    return pltpu.with_memory_space_constraint(x, pltpu.HBM)


def prepare_kernel(step_gain, slabs, vol_hbm, start_hbm, len_hbm, slot_hbm, relax_ref,
                   low_ref, high_ref, table_ref,
                   first, last, start_ref, len_ref, slot_ref, sem):
    rows = vol_hbm.shape[0]
    det = table_ref.shape[1]
    tile = first.shape[0]
    pairs = [
        (start_hbm, start_ref),
        (len_hbm, len_ref),
        (slot_hbm, slot_ref),
        (vol_hbm.at[0:tile], first),
        (vol_hbm.at[rows - tile : rows], last),
    ]
    copies = [pltpu.make_async_copy(*pair, sem.at[i]) for i, pair in enumerate(pairs)]
    for copy in copies:
        copy.start()
    for copy in copies[:3]:
        copy.wait()
    orient = lax.axis_index("orient")
    slab = lax.axis_index("slab")
    lanes = lax.broadcasted_iota(jnp.int32, (1, det), 1)

    def line(flag):
        return jnp.full((1, det), jnp.where(flag, 1.0, 0.0), f32)

    for k in range(8):
        begin = start_ref[k]
        inside = (lanes >= begin) & (lanes < begin + len_ref[k])
        table_ref[MASK + k : MASK + k + 1, :] = jnp.where(inside, 1.0, 0.0)
    for s in range(FRAMES):
        image = slot_ref[jnp.bitwise_xor(orient, s)]
        refl = jnp.right_shift(image, 2)
        for k in range(8):
            wanted = k * FRAMES + jnp.bitwise_and(orient + k, FRAMES - 1)
            table_ref[HELD + 8 * s + k : HELD + 8 * s + k + 1, :] = line(image == wanted)
            table_ref[PICK + 8 * s + k : PICK + 8 * s + k + 1, :] = line(refl == k)
    mine = slot_ref[orient]
    source = jnp.bitwise_and(jnp.bitwise_xor(mine - jnp.right_shift(mine, 2), orient), FRAMES - 1)
    for s in range(FRAMES):
        table_ref[FROM + s : FROM + s + 1, :] = line(source == s)
    table_ref[SCALE : SCALE + 1, :] = jnp.full((1, det), relax_ref[0] * step_gain, f32)
    table_ref[BOUND : BOUND + 1, :] = line(slab != slabs - 1) * huber_delta
    table_ref[BOUND + 1 : BOUND + 2, :] = line(slab != 0) * huber_delta
    table_ref[BOUND + 2 : BOUND + 3, :] = line(slab < 0)
    for copy in copies[3:]:
        copy.wait()
    high_ref[...] = first[0:2, :]
    low_ref[...] = last[tile - 2 :, :]


def prepare(vol, start, length, slot_image, relax, det, step_gain, slabs):
    _, cells = vol.shape
    edge = jax.ShapeDtypeStruct((2, cells), bf16)
    return pl.pallas_call(
        lambda *refs: prepare_kernel(step_gain, slabs, *refs),
        in_specs=[HBM] * 4 + [SMEM],
        out_specs=(VMEM,) * 3,
        out_shape=(edge, edge, jax.ShapeDtypeStruct((TABLE, det), f32)),
        scratch_shapes=[
            pltpu.VMEM((HALO, cells), bf16),
            pltpu.VMEM((HALO, cells), bf16),
            pltpu.SMEM(start.shape, jnp.int32),
            pltpu.SMEM(length.shape, jnp.int32),
            pltpu.SMEM(slot_image.shape, jnp.int32),
            pltpu.SemaphoreType.DMA((5,)),
        ],
        compiler_params=pltpu.CompilerParams(vmem_limit_bytes=SMALL),
        cost_estimate=pl.CostEstimate(flops=40 << 30, transcendentals=0, bytes_accessed=1 << 20),
        name="prepare",
    )(*(keep(x) for x in (vol, start, length, slot_image)), relax)


def pack_kernel(low_ref, high_ref, *refs):
    gathered, near_ref, far_ref = refs[:FRAMES], refs[FRAMES], refs[FRAMES + 1]
    rows = gathered[0].shape[0]
    low = jnp.concatenate([low_ref[...]] + [g[rows - 2 :, :].astype(bf16) for g in gathered], axis=1)
    high = jnp.concatenate([high_ref[...]] + [g[0:2, :].astype(bf16) for g in gathered], axis=1)
    even = jnp.bitwise_and(lax.axis_index("slab"), 1) == 0

    @pl.when(even)
    def _():
        near_ref[...] = low
        far_ref[...] = high

    @pl.when(jnp.logical_not(even))
    def _():
        near_ref[...] = high
        far_ref[...] = low


def pack(low, high, gathered):
    shape = jax.ShapeDtypeStruct((2, low.shape[1] + FRAMES * gathered[0].shape[1]), bf16)
    return pl.pallas_call(
        pack_kernel,
        in_specs=[VMEM] * (2 + FRAMES),
        out_specs=(VMEM, VMEM),
        out_shape=(shape, shape),
        compiler_params=pltpu.CompilerParams(vmem_limit_bytes=SMALL),
        name="pack",
    )(low, high, *gathered)


def halo_rows(near, far, even):
    below = jnp.where(even, near, far)
    above = jnp.where(even, far, near)
    zeros = jnp.zeros((HALO - 4, near.shape[1]), bf16)
    return jnp.concatenate([below, zeros, above], axis=0)


def relay(rays_ref, table_ref, flat_ref, begin, count, skip):
    refl, det = rays_ref.shape[1:]
    low = lax.broadcasted_iota(jnp.int32, (1, det), 1) < det // 2
    low_block = jnp.broadcast_to(low, (PIECE, det))
    stay = []
    for k in range(MASK, MASK + refl, 2):
        line = jnp.where(low, table_ref[k : k + 1, :], table_ref[k + 1 : k + 2, :])
        stay.append(jnp.broadcast_to(line.astype(bf16), (PIECE, det)) > 0.5)
    for j in range(begin, begin + count, PIECE):
        flat = rays_ref[skip + j : skip + j + PIECE].reshape(PIECE, refl * det)
        for p, keeps in enumerate(stay):
            first = flat[:, 2 * p * det : (2 * p + 1) * det]
            second = flat[:, (2 * p + 1) * det : (2 * p + 2) * det]
            straight = jnp.where(low_block, first, second)
            crossed = jnp.where(low_block, second, first)
            flat_ref[j : j + PIECE, p * det : (p + 1) * det] = jnp.where(
                keeps, straight, pltpu.roll(crossed, det // 2, 1)
            )


def relay_kernel(rays_ref, table_ref, flat_ref):
    relay(rays_ref, table_ref, flat_ref, 0, flat_ref.shape[0], 0)


def relay_ahead(rays, table):
    _, refl, det = rays.shape
    return pl.pallas_call(
        relay_kernel,
        in_specs=[VMEM, VMEM],
        out_specs=VMEM,
        out_shape=pltpu.VMEM((EARLY, refl * det // 2), bf16),
        compiler_params=pltpu.CompilerParams(vmem_limit_bytes=SMALL),
        name="relay",
    )(rays, table)


def project_kernel(vol_hbm, near_ref, far_ref, ahead_ref, rays_ref, table_ref, proj_ref, flat_ref, vol_ref, acc, sem):
    rows, cells = vol_hbm.shape
    refl, det = rays_ref.shape[1:]
    early = ahead_ref.shape[0]
    copy = pltpu.make_async_copy(vol_hbm, vol_ref.at[0:rows], sem)
    copy.start()
    even = jnp.bitwise_and(lax.axis_index("slab"), 1) == 0
    vol_ref[rows:, :] = halo_rows(near_ref[:, 0:cells], far_ref[:, 0:cells], even)
    for begin in range(0, cells - early, CHUNK):
        relay(rays_ref, table_ref, flat_ref, begin, CHUNK, early)
        if begin == 0:
            copy.wait()
            acc[...] = jnp.dot(vol_ref[:, 0:early], ahead_ref[...], preferred_element_type=f32)
        acc[...] += jnp.dot(
            vol_ref[:, early + begin : early + begin + CHUNK],
            flat_ref[begin : begin + CHUNK, :],
            preferred_element_type=f32,
        )
    low = lax.broadcasted_iota(jnp.int32, (1, det), 1) < det // 2
    for k in range(0, refl, 2):
        both = acc[:, k // 2 * det : (k // 2 + 1) * det]
        swapped = pltpu.roll(both, det // 2, 1)
        proj_ref[k] = jnp.where(low, both, swapped) * table_ref[MASK + k : MASK + k + 1, :]
        proj_ref[k + 1] = jnp.where(low, swapped, both) * table_ref[MASK + k + 1 : MASK + k + 2, :]


def project(vol, near, far, ahead, rays, table):
    rows, cells = vol.shape
    refl, det = rays.shape[1:]
    ext = rows + HALO
    return pl.pallas_call(
        project_kernel,
        in_specs=[HBM] + [VMEM] * 5,
        out_specs=(VMEM, VMEM, VMEM),
        out_shape=(
            jax.ShapeDtypeStruct((refl, ext, det), f32),
            pltpu.VMEM((cells - EARLY, refl * det // 2), bf16),
            pltpu.VMEM((ext, cells), bf16),
        ),
        scratch_shapes=[pltpu.VMEM((ext, refl * det // 2), f32), pltpu.SemaphoreType.DMA],
        compiler_params=pltpu.CompilerParams(vmem_limit_bytes=8 << 20),
        name="project",
    )(keep(vol), near, far, ahead, rays, table)


def combine_kernel(proj_ref, table_ref, near_ref, far_ref, *refs):
    gathered, part_ref = refs[:FRAMES], refs[FRAMES]
    _, det = gathered[0].shape
    cells = near_ref.shape[1] - FRAMES * det
    even = jnp.bitwise_and(lax.axis_index("slab"), 1) == 0
    halo = halo_rows(near_ref[:, cells:], far_ref[:, cells:], even).astype(f32)
    images = [
        jnp.concatenate([ref[...], halo[:, s * det : (s + 1) * det]], axis=0)
        for s, ref in enumerate(gathered)
    ]
    for k in range(proj_ref.shape[0]):
        part = proj_ref[k]
        for s in range(FRAMES):
            row = HELD + 8 * s + k
            part = part - table_ref[row : row + 1, :] * images[s]
        part_ref[k] = part.astype(bf16)


def combine(proj, table, near, far, gathered):
    return pl.pallas_call(
        combine_kernel,
        in_specs=[VMEM] * (4 + FRAMES),
        out_specs=VMEM,
        out_shape=jax.ShapeDtypeStruct(proj.shape, bf16),
        compiler_params=pltpu.CompilerParams(vmem_limit_bytes=SMALL),
        name="combine",
    )(proj, table, near, far, *gathered)


def total_kernel(pieces_ref, out_ref):
    count = pieces_ref.shape[0]
    total = pieces_ref[0].astype(f32)
    for i in range(1, count):
        total = total + pieces_ref[i].astype(f32)
    own = (-total).astype(bf16)
    for i in range(count):
        out_ref[i] = own


def total(pieces):
    return pl.pallas_call(
        total_kernel,
        in_specs=[VMEM],
        out_specs=VMEM,
        out_shape=jax.ShapeDtypeStruct(pieces.shape, bf16),
        compiler_params=pltpu.CompilerParams(vmem_limit_bytes=SMALL),
        name="total",
    )(pieces)


def pick_kernel(img_ref, table_ref, *outs):
    rows = outs[0].shape[0]
    for s in range(FRAMES):
        image = jnp.zeros(outs[0].shape, f32)
        for k in range(img_ref.shape[0]):
            row = PICK + 8 * s + k
            image = image + table_ref[row : row + 1, :] * img_ref[k, 0:rows, :].astype(f32)
        outs[s][...] = image.astype(bf16)


def pick(img, table, rows):
    shape = jax.ShapeDtypeStruct((rows, img.shape[2]), bf16)
    return pl.pallas_call(
        pick_kernel,
        in_specs=[VMEM, VMEM],
        out_specs=(VMEM,) * FRAMES,
        out_shape=(shape,) * FRAMES,
        compiler_params=pltpu.CompilerParams(vmem_limit_bytes=SMALL),
        name="pick",
    )(img, table)


def choose_kernel(table_ref, *refs):
    image = jnp.zeros(refs[0].shape, f32)
    for s in range(FRAMES):
        image = image + table_ref[FROM + s : FROM + s + 1, :] * refs[s][...].astype(f32)
    refs[FRAMES][...] = image


def choose(table, images):
    return pl.pallas_call(
        choose_kernel,
        in_specs=[VMEM] * (1 + FRAMES),
        out_specs=VMEM,
        out_shape=jax.ShapeDtypeStruct(images[0].shape, f32),
        compiler_params=pltpu.CompilerParams(vmem_limit_bytes=SMALL),
        name="choose",
    )(table, *images)


def update_kernel(img_ref, table_ref, ahead_ref, flat_ref, vol_ref, out_hbm, dbuf, fbuf, obuf, osem):
    refl, ext, det = img_ref.shape
    cells = vol_ref.shape[1]
    rows = ext - HALO
    slots = dbuf.shape[0]
    tiles = slots // 2
    chunk = tiles * det
    steps = cells // chunk
    sends = osem.shape[0]

    low = lax.broadcasted_iota(jnp.int32, (1, det), 1) < det // 2
    parts = []
    for k in range(0, refl, 2):
        first = img_ref[k].astype(f32) * table_ref[MASK + k : MASK + k + 1, :]
        second = img_ref[k + 1].astype(f32) * table_ref[MASK + k + 1 : MASK + k + 2, :]
        straight = jnp.where(low, first, second)
        crossed = jnp.where(low, second, first)
        parts.append((straight + pltpu.roll(crossed, det // 2, 1)).astype(bf16))
    img = jnp.concatenate(parts, axis=1)
    scale = table_ref[SCALE : SCALE + 1, 0:1]

    place = lax.broadcasted_iota(jnp.int32, (ext, det), 0)
    bound = jnp.where(
        place == rows + 7,
        table_ref[BOUND : BOUND + 1, :],
        jnp.where(place == 7, table_ref[BOUND + 1 : BOUND + 2, :], huber_delta),
    )
    zeros = jnp.zeros((8, det), f32)
    for q in range(slots):
        dbuf[q, 0:8] = zeros
        dbuf[q, 8 + ext :] = zeros
        fbuf[q, 0:8] = zeros

    def psi(t, first):
        limit = bound[first : first + t.shape[0]]
        return jnp.minimum(jnp.maximum(t, -limit), limit)

    def backproject(i):
        at = slice(i * chunk, (i + 1) * chunk)
        early = ahead_ref.shape[0]
        if i * chunk < early:
            flat = ahead_ref[at, :]
        else:
            flat = flat_ref[i * chunk - early : (i + 1) * chunk - early, :]
        gradient = lax.dot_general(img, flat, (((1,), (1,)), ((), ())), preferred_element_type=f32)
        density = vol_ref[:, at].astype(f32) + scale * gradient
        for t in range(tiles):
            q = (i * tiles + t) % slots
            lanes = slice(t * det, (t + 1) * det)
            dbuf[q, 8:16] = density[ext - 8 :, lanes]
            dbuf[q, 16 : 8 + ext] = density[0 : ext - 8, lanes]

    def out_copy(j):
        at = slice(j * (cells // sends), (j + 1) * (cells // sends))
        return pltpu.make_async_copy(obuf.at[:, at], out_hbm.at[:, at], osem.at[j])

    def smooth(i):
        for t in range(tiles):
            q = (i * tiles + t) % slots
            here = dbuf[q, 8 : 8 + ext]
            flux = psi(dbuf[q, 9 : 9 + ext] - here, 0)
            fbuf[q, 8 : 8 + ext] = flux
            once = here + sweep_rate * (flux - fbuf[q, 7 : 7 + ext])
            dbuf[q, 8 : 8 + ext] = once
            fbuf[q, 8 : 16 + rows] = psi(dbuf[q, 9 : 17 + rows] - once[0 : 8 + rows], 0)
            net = fbuf[q, 16 : 16 + rows] - fbuf[q, 15 : 15 + rows]
            at = slice(i * chunk + t * det, i * chunk + (t + 1) * det)
            obuf[:, at] = (once[8 : 8 + rows] + sweep_rate * net).astype(bf16)
        if (i + 1) * sends % steps == 0:
            out_copy((i + 1) * sends // steps - 1).start()

    backproject(0)
    for i in range(1, steps):
        backproject(i)
        smooth(i - 1)
    smooth(steps - 1)
    for j in range(sends):
        out_copy(j).wait()


def update(img, table, ahead, flat, vol_ext, chunk=256, sends=16):
    ext, cells = vol_ext.shape
    rows = ext - HALO
    det = img.shape[2]
    slot = pltpu.VMEM((2 * chunk // det, ext + 16, det), f32)
    return pl.pallas_call(
        update_kernel,
        in_specs=[VMEM] * 5,
        out_specs=HBM,
        out_shape=jax.ShapeDtypeStruct((rows, cells), bf16),
        scratch_shapes=[slot, slot, pltpu.VMEM((rows, cells), bf16), pltpu.SemaphoreType.DMA((sends,))],
        compiler_params=pltpu.CompilerParams(vmem_limit_bytes=8 << 20),
        name="update",
    )(img, table, ahead, flat, vol_ext)


def local(volume, rays, band_start, band_len, slot_image, measured, relax):
    cells, refl, det = rays.shape
    rows = volume.shape[1]
    slabs = lax.axis_size("slab")
    orients = lax.axis_size("orient")
    members = orients // FRAMES
    classes = [[g * FRAMES + q for g in range(members)] for q in range(FRAMES)]
    vol = volume[0]
    meas = measured[0]
    step_gain = math.sqrt(cells * orients / (FRAMES * refl * det))

    swaps = [[(o, o ^ s) for o in range(orients)] for s in range(FRAMES)]
    gathered = [meas] + [lax.ppermute(meas, "orient", swaps[s]) for s in range(1, FRAMES)]
    low, high, table = prepare(
        vol, band_start[:, 0], band_len[:, 0], slot_image, relax, det, step_gain, slabs
    )
    near, far = pack(low, high, gathered)

    near = lax.ppermute(near, "slab", [(i, i ^ 1) for i in range(slabs)])
    far = lax.ppermute(far, "slab", [(i, slabs - 1 - i) for i in range(slabs)])
    ahead = relay_ahead(rays, table)
    proj, flat, vol_ext = project(vol, near, far, ahead, rays, table)

    part = combine(proj, table, near, far, gathered)
    pieces = lax.all_to_all(part, "orient", 0, 0, axis_index_groups=classes, tiled=True)
    images = lax.all_to_all(total(pieces), "orient", 0, 0, axis_index_groups=classes, tiled=True)

    picked = pick(images, table, rows)
    arrived = [picked[0]] + [lax.ppermute(picked[s], "orient", swaps[s]) for s in range(1, FRAMES)]
    updated = update(images, table, ahead, flat, vol_ext)
    residual = choose(table, arrived)
    return (updated[None], residual[None])


def solution(mesh):
    placed = (
        P("orient", "slab", None),
        P(),
        P(None, "orient"),
        P(None, "orient"),
        P(),
        P("orient", "slab", None),
        P("orient"),
    )
    return jax.shard_map(
        local,
        mesh=mesh,
        in_specs=placed,
        out_specs=(P("orient", "slab", None), P("orient", "slab", None)),
        check_vma=False,
    )
```
